32 devices in a mesh: fsdp: 4 (over y, x), context: 4 (over z), tensor: 2 (over core).
Axes of the slice: x: 2, y: 2, z: 4, core: 2. Of those that a mesh axis runs over, the one named last changes fastest.
Arguments:
- tokens: bfloat16 [2, 4096, 2048], P(None, ('fsdp', 'context')), may hold values from -6 to 6
- cotangent: bfloat16 [2, 4096, 2048], P(None, ('fsdp', 'context')), may hold values from -6 to 6
- seg_parent: int32 [2, 32], P(None, 'fsdp'), may hold values from -1 to 7, as said below
- positions: int32 [2, 4096], P(None, 'fsdp'), may hold values from 0 to 895, as said below
- norm_gain: bfloat16 [2, 2048], P(None, 'fsdp'), may hold values from 0.5 to 1.5
- norm_bias: bfloat16 [2, 2048], P(None, 'fsdp'), may hold values from -1.1953125 to 1.1953125
- w_qkv: bfloat16 [3, 2048, 2048], P(None, 'fsdp', 'tensor'), may hold values from -0.125 to 0.125
- bias_qv: bfloat16 [2, 2048], P(None, ('tensor', 'fsdp')), may hold values from -1.1953125 to 1.1953125
- w_out: bfloat16 [2048, 2048], P('tensor', 'fsdp'), may hold values from -0.25 to 0.25
- bias_out: bfloat16 [2048], P('fsdp'), may hold values from -1.1953125 to 1.1953125
- w_up: bfloat16 [2048, 8192], P('fsdp', 'tensor'), may hold values from -0.125 to 0.125
- bias_up: bfloat16 [8192], P(('tensor', 'fsdp')), may hold values from -1.1953125 to 1.1953125
- w_down: bfloat16 [8192, 2048], P('tensor', 'fsdp'), may hold values from -0.0625 to 0.0625
- bias_down: bfloat16 [2048], P('fsdp'), may hold values from -1.1953125 to 1.1953125
Outputs:
- layer_out: bfloat16 [2, 4096, 2048], P(None, ('fsdp', 'context'))
- grad_tokens: bfloat16 [2, 4096, 2048], P(None, ('fsdp', 'context'))
- grad_norm_gain: float32 [2, 2048], P(None, 'fsdp')
- grad_norm_bias: float32 [2, 2048], P(None, 'fsdp')
- grad_w_qkv: float32 [3, 2048, 2048], P(None, 'fsdp', 'tensor')
- grad_bias_qv: float32 [2, 2048], P(None, ('tensor', 'fsdp'))
- grad_w_out: float32 [2048, 2048], P('tensor', 'fsdp')
- grad_bias_out: float32 [2048], P('fsdp')
- grad_w_up: float32 [2048, 8192], P('fsdp', 'tensor')
- grad_bias_up: float32 [8192], P(('tensor', 'fsdp'))
- grad_w_down: float32 [8192, 2048], P('tensor', 'fsdp')
- grad_bias_down: float32 [2048], P('fsdp')
The draws below stay inside these ranges and needn't reach their ends.
Inputs may be any that keep to these rules, and one draw needn't show every extreme that they name: `seg_parent`: each micro-batch holds 4 trees of 8 entries; a tree is a trunk of 5 segments in a chain from a root, 1 branches whose parent is the trunk's last segment, and 2 leaves whose parent is each branch; which slot holds which segment is a permutation drawn from the seed for each tree. `positions`: A token's position is the depth of its segment in its tree times 128 plus its place within the segment.
All inputs are finite; a program needn't handle non-finite values.
Results may differ from the reference program's by a relative error of at most 0.02.
Values may be sent and summed in bfloat16 or wider, within the bound.
No kernel may reach another device: no remote copies, remote signals or barrier semaphores. Data moves between devices by JAX's collectives and lax.ppermute only.
A program may use at most 384 MiB of HBM per device.

```python
import jax
import jax.numpy as jnp
import numpy as np
from jax import lax

D = 2048
HEADS = 32
HEAD_DIM = 64
FF = 8192
SEG = 128
TRUNK_SEGS = 5
BRANCHES = 1
LEAVES = 2
MICRO = 2
TREE_SEGS = 8
GROUP_TOK = 1024
ROWS = 4096
FOREST = 32
GROUPS = 8


def tree_tables():
    parent_tree = []
    depth_tree = []
    for trunk_index in range(TRUNK_SEGS):
        parent_tree.append(trunk_index - 1)
        depth_tree.append(trunk_index)
    for branch_index in range(BRANCHES):
        parent_tree.append(TRUNK_SEGS - 1)
        depth_tree.append(TRUNK_SEGS)
    for branch_index in range(BRANCHES):
        for leaf_index in range(LEAVES):
            parent_tree.append(TRUNK_SEGS + branch_index)
            depth_tree.append(TRUNK_SEGS + 1)
    return (np.array(parent_tree, np.int32), np.array(depth_tree, np.int32))


def tree_layout(key):
    parent_tree, depth_tree = tree_tables()
    tree_keys = jax.random.split(jax.random.fold_in(key, 7), GROUPS)
    slot_of = jax.vmap(lambda one_key: jax.random.permutation(one_key, TREE_SEGS))(tree_keys).astype(jnp.int32)
    parent_slot = jnp.where(jnp.asarray(parent_tree)[None, :] < 0, -1, slot_of[:, np.maximum(parent_tree, 0)])
    tree_rows = jnp.arange(GROUPS, dtype=jnp.int32)[:, None] * jnp.ones((1, TREE_SEGS), jnp.int32)
    parents = jnp.zeros((GROUPS, TREE_SEGS), jnp.int32).at[tree_rows, slot_of].set(parent_slot)
    depth_rows = jnp.broadcast_to(jnp.asarray(depth_tree)[None, :], (GROUPS, TREE_SEGS))
    depths = jnp.zeros((GROUPS, TREE_SEGS), jnp.int32).at[tree_rows, slot_of].set(depth_rows)
    return (parents, depths)


def draw_seg_parent(key, part):
    parents, depths = tree_layout(key)
    return parents.reshape(MICRO, FOREST)


def draw_positions(key, part):
    parents, depths = tree_layout(key)
    places = depths[:, :, None] * SEG + jnp.arange(SEG, dtype=jnp.int32)[None, None, :]
    return places.reshape(MICRO, ROWS)


def strengthened(result, key, source, target, parts, factor):
    owner, partner = [(jnp.arange(result.shape[axis_at]) // (result.shape[axis_at] // parts)).reshape([-1 if axis == axis_at else 1 for axis in range(result.ndim)]) for axis_at in (source, target)]
    chosen = jax.random.permutation(key, parts)[partner]
    strong = (owner == chosen) | (owner == (partner + parts // 2) % parts)
    return jnp.where(strong, factor * result, result)


def level_of(rng, dims, shards, least, top_value):
    loudness = 1.0
    for axis_at, blocks in shards:
        heights = jax.random.uniform(jax.random.fold_in(jax.random.fold_in(rng, 6), axis_at), (blocks,), jnp.float32, least / len(shards), top_value / len(shards))
        loudness = loudness * jnp.repeat(jnp.exp(heights), dims[axis_at] // blocks).reshape((-1,) + (1,) * (len(dims) - 1 - axis_at))
    return loudness


def scatter_about(stream_key, dims, deviation, reach, cuts=(), kind=jnp.bfloat16):
    level = level_of(stream_key, dims, cuts, -0.22, 0.18) if cuts else 1.0
    result = jax.random.normal(stream_key, dims, jnp.float32) * deviation * level
    return jnp.minimum(jnp.maximum(result, -reach), reach).astype(kind)


def gaussian_with(own_key, dims, spread, reach, cuts, heavy, held_as=jnp.bfloat16):
    result = spread * jax.random.normal(own_key, dims, jnp.float32)
    if cuts:
        result = result * level_of(own_key, dims, cuts, -0.22, 0.18)
    return jnp.clip(strengthened(result, jax.random.fold_in(own_key, 3), *heavy), -reach, reach).astype(held_as)


def setup_inputs(seed: int = 0) -> dict:
    key_of = jax.random.split(jax.random.key(seed), 15)
    return {
        "tokens": scatter_about(key_of[0], (MICRO, ROWS, D), 1.0, 6.0, ((1, 16),)),
        "cotangent": gaussian_with(key_of[1], (MICRO, ROWS, D), 1.0, 6.0, ((1, 16),), (1, 2, 16, 2.0)),
        "seg_parent": draw_seg_parent(jax.random.fold_in(key_of[14], 71), 0),
        "positions": draw_positions(jax.random.fold_in(key_of[14], 71), 0),
        "norm_gain": jnp.clip(1.0 + 0.1 * jax.random.normal(key_of[4], (2, D), jnp.float32), 0.5, 1.5).astype(jnp.bfloat16),
        "norm_bias": scatter_about(key_of[5], (2, D), 0.2, 1.1953125, ((1, 4),)),
        "w_qkv": scatter_about(key_of[6], (3, D, D), D ** -0.5, 0.125, ((1, 4), (2, 2))),
        "bias_qv": scatter_about(key_of[7], (2, D), 0.2, 1.1953125, ((1, 8),)),
        "w_out": scatter_about(key_of[8], (D, D), (D // 4) ** -0.5, 0.25, ((0, 2), (1, 4))),
        "bias_out": scatter_about(key_of[9], (D,), 0.2, 1.1953125, ((0, 4),)),
        "w_up": scatter_about(key_of[10], (D, FF), D ** -0.5, 0.125, ((0, 4), (1, 2))),
        "bias_up": scatter_about(key_of[11], (FF,), 0.2, 1.1953125, ((0, 8),)),
        "w_down": scatter_about(key_of[12], (FF, D), FF ** -0.5, 0.0625, ((0, 2), (1, 4))),
        "bias_down": scatter_about(key_of[13], (D,), 0.2, 1.1953125, ((0, 4),)),
    }


@jax.custom_vjp
def low(v):
    return lax.optimization_barrier(v.astype(jnp.bfloat16)).astype(jnp.float32)

@jax.custom_vjp
def low_back(v):
    return v

def low_keep(v):
    return (low(v), None)

def low_pass(kept, grad):
    return (grad,)

def back_keep(v):
    return (v, None)

def back_low(kept, grad):
    return (low(grad),)
low.defvjp(low_keep, low_pass)
low_back.defvjp(back_keep, back_low)
HIGHEST_DOT = lax.Precision.HIGHEST

def norm_rows(values_in, gain, shift):
    row_mean = lax.optimization_barrier(jnp.mean(values_in, axis=-1, keepdims=True))
    centred = values_in - row_mean
    variance = lax.optimization_barrier(jnp.mean(centred * centred, axis=-1, keepdims=True))
    return centred * lax.rsqrt(variance + 1e-05) * gain + shift

def ancestry_table(parents):
    slot_ids = jnp.arange(parents.shape[0], dtype=jnp.int32)
    parent_step = (parents[:, None] == slot_ids[None, :]).astype(jnp.float32)
    reach_now = jnp.eye(parents.shape[0], dtype=jnp.float32)
    reached = reach_now
    for depth_step in range(TRUNK_SEGS + 1):
        reach_now = jnp.dot(reach_now, parent_step, precision=HIGHEST_DOT)
        reached = reached + reach_now
    return reached > 0.5

def head_attention(queries, key_rows, values, head_slope, allowed, offsets):
    scores = jnp.dot(queries, key_rows.T, precision=HIGHEST_DOT) * HEAD_DIM ** (-0.5) + head_slope * offsets
    scores = jnp.where(allowed, low_back(scores), -1e+30)
    highest = lax.optimization_barrier(jnp.max(scores, axis=-1, keepdims=True))
    raised = jnp.exp(scores - highest)
    probabilities = low(raised / lax.optimization_barrier(jnp.sum(raised, axis=-1, keepdims=True)))
    return jnp.dot(probabilities, values, precision=HIGHEST_DOT)

def head_split(matrix):
    return matrix.reshape(GROUP_TOK, HEADS, HEAD_DIM).transpose(1, 0, 2)

def tree_forward(params, hidden_in, parents, places):
    norm_gains, norm_shifts, w_qkv, bias_qv, w_out, bias_out, w_up, bias_up, w_down, bias_down = params
    normed = low(norm_rows(hidden_in, norm_gains[0], norm_shifts[0]))
    queries = low_back(low(jnp.dot(normed, w_qkv[0], precision=HIGHEST_DOT) + bias_qv[0]))
    key_rows = low_back(low(jnp.dot(normed, w_qkv[1], precision=HIGHEST_DOT)))
    values = low_back(low(jnp.dot(normed, w_qkv[2], precision=HIGHEST_DOT) + bias_qv[1]))
    ancestry = ancestry_table(parents)
    slot_of = jnp.arange(GROUP_TOK, dtype=jnp.int32) // SEG
    allowed = ancestry[slot_of][:, slot_of] & (places[None, :] <= places[:, None])
    offsets = (places[None, :] - places[:, None]).astype(jnp.float32)
    slopes = jnp.exp2(-8.0 * jnp.arange(1, HEADS + 1, dtype=jnp.float32) / HEADS)

    def per_head(packed):
        return head_attention(packed[0], packed[1], packed[2], packed[3], allowed, offsets)
    attended = lax.map(jax.checkpoint(per_head), (head_split(queries), head_split(key_rows), head_split(values), slopes))
    attended = low_back(low(attended.transpose(1, 0, 2).reshape(GROUP_TOK, D)))
    branch = low_back(jnp.dot(attended, w_out, precision=HIGHEST_DOT) + bias_out)
    middle = hidden_in + branch
    normed_two = low(norm_rows(middle, norm_gains[1], norm_shifts[1]))
    pre_act = low_back(jnp.dot(normed_two, w_up, precision=HIGHEST_DOT) + bias_up)
    activated = low(jax.nn.gelu(pre_act, approximate=False))
    return middle + (jnp.dot(activated, w_down, precision=HIGHEST_DOT) + bias_down)

def reference(tokens, cotangent, seg_parent, positions, norm_gain, norm_bias, w_qkv, bias_qv, w_out, bias_out, w_up, bias_up, w_down, bias_down):
    params = tuple((weight.astype(jnp.float32) for weight in (norm_gain, norm_bias, w_qkv, bias_qv, w_out, bias_out, w_up, bias_up, w_down, bias_down)))
    inputs = tokens.astype(jnp.float32).reshape(GROUPS, GROUP_TOK, D)
    cotangents = cotangent.astype(jnp.float32).reshape(GROUPS, GROUP_TOK, D)
    parents_all = seg_parent.reshape(GROUPS, TREE_SEGS)
    places_all = positions.reshape(GROUPS, GROUP_TOK)

    def forward(params_now, inputs_now):

        def one_tree(unused_carry, packed):
            hidden_now, parents, places = packed
            checked = jax.checkpoint(lambda params_in, hidden_in: tree_forward(params_in, hidden_in, parents, places))
            return (unused_carry, checked(params_now, hidden_now))
        unused_final, outputs_now = lax.scan(one_tree, jnp.zeros((), jnp.float32), (inputs_now, parents_all, places_all))
        return outputs_now
    outputs, pullback = jax.vjp(forward, params, inputs)
    grad_params, grad_inputs = pullback(cotangents)
    layer_out = outputs.reshape(MICRO, ROWS, D).astype(jnp.bfloat16)
    grad_tokens = grad_inputs.reshape(MICRO, ROWS, D).astype(jnp.bfloat16)
    return (layer_out, grad_tokens, grad_params[0], grad_params[1], grad_params[2], grad_params[3], grad_params[4], grad_params[5], grad_params[6], grad_params[7], grad_params[8], grad_params[9])
```

```python
from functools import partial

import jax
import jax.numpy as jnp
from jax import lax
from jax.experimental import pallas as pl
from jax.experimental.pallas import tpu as pltpu
from jax.sharding import PartitionSpec as P

HEADS = 32
HEAD_DIM = 64
SEG = 128
TREE_SEGS = 8
LAST_DEPTH = 6
MICRO = 2
PAIR = 2 * HEAD_DIM
NEG_FILL = -1e30
F32 = jnp.float32
BF16 = jnp.bfloat16


def dot_nn(left, right):
    return lax.dot_general(left, right, (((1,), (0,)), ((), ())), preferred_element_type=F32)


def dot_tn(left, right):
    return lax.dot_general(left, right, (((0,), (0,)), ((), ())), preferred_element_type=F32)


def dot_nt(left, right):
    return lax.dot_general(left, right, (((1,), (1,)), ((), ())), preferred_element_type=F32)


def swap_cores(value):
    return lax.ppermute(value, "tensor", [(0, 1), (1, 0)])


def xor_send(value, step):
    size = lax.axis_size("fsdp")
    return lax.ppermute(value, "fsdp", [(i, i ^ step) for i in range(size)])


def ring_send(value, step):
    size = lax.axis_size("context")
    return lax.ppermute(value, "context", [(i, (i + step) % size) for i in range(size)])


def line_gather(value):
    size = lax.axis_size("context")
    index = lax.axis_index("context")
    upward, downward = [value], [value]
    for step in range(1, size):
        upward.append(
            lax.ppermute(upward[-1], "context", [(i, i + 1) for i in range(step - 1, size - 1)])
        )
        downward.append(
            lax.ppermute(downward[-1], "context", [(i + 1, i) for i in range(0, size - step)])
        )
    blocks = [value]
    for step in range(1, size):
        blocks.append(jnp.where(index + step < size, downward[step], upward[size - step]))
    return blocks


def gather_rows(value):
    return [value] + [xor_send(value, k) for k in range(1, lax.axis_size("fsdp"))]


def place(pieces, axis):
    index = lax.axis_index("fsdp")
    width = pieces[0].shape[axis]
    shape = list(pieces[0].shape)
    shape[axis] = width * len(pieces)
    whole = jnp.zeros(shape, pieces[0].dtype)
    for k, piece in enumerate(pieces):
        whole = lax.dynamic_update_slice_in_dim(whole, piece, (index ^ k) * width, axis)
    return whole


def pick(whole, k, axis):
    width = whole.shape[axis] // lax.axis_size("fsdp")
    return lax.dynamic_slice_in_dim(whole, (lax.axis_index("fsdp") ^ k) * width, width, axis)


def exchange(whole, axis):
    blocks = [pick(whole, 0, axis)]
    for k in range(1, lax.axis_size("fsdp")):
        blocks.append(xor_send(pick(whole, k, axis), k))
    return blocks


def sum_blocks(own, pieces):
    total = own.astype(F32)
    for k, piece in enumerate(pieces, 1):
        total = total + xor_send(piece.astype(BF16), k).astype(F32)
    return total


def head_lanes(rows):
    return lax.broadcasted_iota(jnp.int32, (rows, PAIR), 1) < HEAD_DIM


def split_heads(value):
    first = head_lanes(value.shape[0])
    zero = jnp.zeros_like(value)
    return jnp.concatenate([jnp.where(first, value, zero), jnp.where(first, zero, value)], axis=0)


def join_heads(stacked):
    first = head_lanes(SEG)
    return jnp.where(first, stacked[:SEG], stacked[SEG:])


def probabilities(stacked_queries, keys, block, slope_a, slope_b):
    width = (block + 1) * SEG
    scores = dot_nt(stacked_queries, keys)
    row = lax.broadcasted_iota(jnp.int32, (2 * SEG, 1), 0)
    column = lax.broadcasted_iota(jnp.int32, (1, width), 1)
    local = jnp.where(row < SEG, row, row - SEG)
    slope = jnp.where(row < SEG, slope_a, slope_b)
    place_row = local + min(block, LAST_DEPTH) * SEG
    place_column = jnp.where(column < (LAST_DEPTH + 1) * SEG, column, column - SEG)
    scores = scores + slope * (place_column - place_row).astype(F32)
    allowed = column <= local + block * SEG
    if block == LAST_DEPTH + 1:
        allowed = allowed & ((column < LAST_DEPTH * SEG) | (column >= (LAST_DEPTH + 1) * SEG))
    scores = jnp.where(allowed, scores, NEG_FILL)
    raised = jnp.exp(scores - jnp.max(scores, axis=-1, keepdims=True))
    return raised * (1.0 / jnp.sum(raised, axis=-1, keepdims=True))


def attention_forward(order, slopes, qkv_ref, out_ref, keys, values):
    pair = pl.program_id(0)
    slope_a, slope_b = slopes[2 * pair], slopes[2 * pair + 1]
    for block in range(TREE_SEGS):
        rows = pl.ds(block * SEG, SEG)
        keys[rows, :] = qkv_ref[order[block], :, PAIR : 2 * PAIR]
        values[rows, :] = qkv_ref[order[block], :, 2 * PAIR : 3 * PAIR]
    for block in range(TREE_SEGS):
        seen = pl.ds(0, (block + 1) * SEG)
        queries = split_heads(qkv_ref[order[block], :, :PAIR] * BF16(HEAD_DIM**-0.5))
        probs = probabilities(queries, keys[seen, :], block, slope_a, slope_b)
        mixed = dot_nn(probs.astype(BF16), values[seen, :])
        out_ref[order[block]] = join_heads(mixed).astype(BF16)


def attention_backward(order, slopes, qkv_ref, grad_ref, out_ref, keys, values, grad_keys, grad_values):
    pair = pl.program_id(0)
    slope_a, slope_b = slopes[2 * pair], slopes[2 * pair + 1]
    for block in range(TREE_SEGS):
        rows = pl.ds(block * SEG, SEG)
        keys[rows, :] = qkv_ref[order[block], :, PAIR : 2 * PAIR]
        values[rows, :] = qkv_ref[order[block], :, 2 * PAIR : 3 * PAIR]
    grad_keys[...] = jnp.zeros_like(grad_keys)
    grad_values[...] = jnp.zeros_like(grad_values)
    for block in range(TREE_SEGS):
        seen = pl.ds(0, (block + 1) * SEG)
        queries = split_heads(qkv_ref[order[block], :, :PAIR] * BF16(HEAD_DIM**-0.5))
        grads = split_heads(grad_ref[order[block]])
        probs = probabilities(queries, keys[seen, :], block, slope_a, slope_b)
        grad_probs = dot_nt(grads, values[seen, :])
        centre = jnp.sum(probs * grad_probs, axis=-1, keepdims=True)
        grad_scores = (probs * (grad_probs - centre)).astype(BF16)
        grad_queries = join_heads(dot_nn(grad_scores, keys[seen, :])) * HEAD_DIM**-0.5
        out_ref[order[block], :, :PAIR] = grad_queries.astype(BF16)
        grad_keys[seen, :] += dot_tn(grad_scores, queries)
        grad_values[seen, :] += dot_tn(probs.astype(BF16), grads)
    for block in range(TREE_SEGS):
        rows = pl.ds(block * SEG, SEG)
        out_ref[order[block], :, PAIR : 2 * PAIR] = grad_keys[rows, :].astype(BF16)
        out_ref[order[block], :, 2 * PAIR : 3 * PAIR] = grad_values[rows, :].astype(BF16)


def block_of(width):
    return pl.BlockSpec((TREE_SEGS, SEG, width), lambda pair, *scalars: (0, 0, pair))


def attend(order, slopes, qkv):
    pairs = qkv.shape[1] // (3 * PAIR)
    rows = TREE_SEGS * SEG
    out = pl.pallas_call(
        attention_forward,
        out_shape=jax.ShapeDtypeStruct((TREE_SEGS, SEG, pairs * PAIR), BF16),
        grid_spec=pltpu.PrefetchScalarGridSpec(
            num_scalar_prefetch=2,
            grid=(pairs,),
            in_specs=[block_of(3 * PAIR)],
            out_specs=block_of(PAIR),
            scratch_shapes=[pltpu.VMEM((rows, PAIR), BF16)] * 2,
        ),
        compiler_params=pltpu.CompilerParams(vmem_limit_bytes=48 << 20),
        cost_estimate=pl.CostEstimate(
            flops=pairs * 8 * rows * rows * PAIR,
            transcendentals=pairs * rows * rows,
            bytes_accessed=8 * rows * pairs * PAIR,
        ),
        name="attend",
    )(order, slopes, qkv.reshape(TREE_SEGS, SEG, -1))
    return out.reshape(rows, pairs * PAIR)


def attend_back(order, slopes, qkv, grad):
    pairs = qkv.shape[1] // (3 * PAIR)
    rows = TREE_SEGS * SEG
    out = pl.pallas_call(
        attention_backward,
        out_shape=jax.ShapeDtypeStruct((TREE_SEGS, SEG, pairs * 3 * PAIR), BF16),
        grid_spec=pltpu.PrefetchScalarGridSpec(
            num_scalar_prefetch=2,
            grid=(pairs,),
            in_specs=[block_of(3 * PAIR), block_of(PAIR)],
            out_specs=block_of(3 * PAIR),
            scratch_shapes=[pltpu.VMEM((rows, PAIR), BF16)] * 2 + [pltpu.VMEM((rows, PAIR), F32)] * 2,
        ),
        compiler_params=pltpu.CompilerParams(vmem_limit_bytes=48 << 20),
        cost_estimate=pl.CostEstimate(
            flops=pairs * 20 * rows * rows * PAIR,
            transcendentals=pairs * rows * rows,
            bytes_accessed=14 * rows * pairs * PAIR,
        ),
        name="attend_back",
    )(order, slopes, qkv.reshape(TREE_SEGS, SEG, -1), grad.reshape(TREE_SEGS, SEG, -1))
    return out.reshape(rows, pairs * 3 * PAIR)


def normalise(rows):
    centred = rows - jnp.mean(rows, axis=-1, keepdims=True)
    scale = lax.rsqrt(jnp.mean(centred * centred, axis=-1, keepdims=True) + 1e-05)
    return centred * scale, scale


def norm_back(unit, scale, gain, upstream):
    weighted = upstream * gain
    centre = jnp.mean(weighted, axis=-1, keepdims=True)
    along = jnp.mean(weighted * unit, axis=-1, keepdims=True)
    return scale * (weighted - centre - unit * along)


def normal_cdf(value):
    return 0.5 * (1.0 + lax.erf(value * 0.7071067811865476))


def normal_pdf(value):
    return 0.3989422804014327 * jnp.exp(-0.5 * value * value)


def both_micros(mine):
    other = swap_cores(mine)
    first = lax.axis_index("tensor") == 0
    return jnp.stack([jnp.where(first, mine, other), jnp.where(first, other, mine)])


def per_device(
    tokens,
    cotangent,
    seg_parent,
    positions,
    norm_gain,
    norm_bias,
    w_qkv,
    bias_qv,
    w_out,
    bias_out,
    w_up,
    bias_up,
    w_down,
    bias_down,
):
    planes, groups = lax.axis_size("context"), lax.axis_size("fsdp")
    plane, group, core = (lax.axis_index(name) for name in ("context", "fsdp", "tensor"))
    rows, width = tokens.shape[1], tokens.shape[2]
    part = width // groups
    half = w_qkv.shape[2]
    columns = half // planes
    pairs = columns // PAIR
    hidden = w_up.shape[1] // groups
    slots = rows // SEG

    mine = lax.dynamic_index_in_dim(tokens, core, 0, keepdims=False)
    mine_cot = lax.dynamic_index_in_dim(cotangent, core, 0, keepdims=False)
    tree = jnp.concatenate(line_gather(mine), axis=0)

    packed = jnp.concatenate(
        [
            norm_gain,
            norm_bias,
            bias_out[None],
            bias_down[None],
            bias_qv.reshape(1, part),
            bias_up.reshape(-1, part),
        ],
        axis=0,
    )
    small = lax.all_gather(packed, ("tensor", "fsdp"), axis=0, tiled=False).astype(F32)
    small = small.reshape(2, groups, packed.shape[0], part)
    spread = lax.dynamic_index_in_dim(small, core, 0, keepdims=False)[:, :6]
    spread = spread.transpose(1, 0, 2).reshape(6, width)
    gain_one, gain_two, shift_one, shift_two, out_shift, down_shift = (
        spread[i : i + 1] for i in range(6)
    )
    head_shift = small[:, :, 6].reshape(2, groups, 2, part // 2).transpose(0, 2, 1, 3)
    head_shift = lax.dynamic_slice_in_dim(
        head_shift.reshape(2, 2, half), plane * columns, columns, 2
    ).reshape(2, 2, pairs, PAIR)
    head_shift = jnp.stack(
        [head_shift[:, 0], jnp.zeros_like(head_shift[:, 0]), head_shift[:, 1]], axis=2
    ).reshape(2, pairs * 3 * PAIR)
    up_shift = lax.dynamic_index_in_dim(small, group, 1, keepdims=False)[:, 7:].reshape(2, hidden)

    def own_first(both):
        return jnp.where(core == 0, both, both[::-1])

    head_shift = own_first(head_shift).reshape(1, -1)
    up_shift = own_first(up_shift)

    chosen = lax.dynamic_slice_in_dim(w_qkv, plane * columns, columns, 2)
    chosen = chosen.reshape(3, part, pairs, PAIR).transpose(1, 2, 0, 3).reshape(part, 3 * columns)
    heads_own = lax.all_gather(chosen, "fsdp", axis=0, tiled=True)
    w_heads = jnp.concatenate([heads_own, swap_cores(heads_own)], axis=1)
    out_own = lax.all_gather(w_out, "fsdp", axis=1, tiled=True)
    out_other = swap_cores(out_own)

    up_own = place(exchange(w_up, 1), 0)
    down_own = place(exchange(w_down, 0), 1)
    up_other, down_other = swap_cores(up_own), swap_cores(down_own)
    all_cot = jnp.concatenate(gather_rows(mine_cot), axis=0)

    depth = lax.dynamic_index_in_dim(positions, core, 0, keepdims=False)[::SEG] // SEG
    depth = jnp.roll(depth, -plane * slots)
    ids = jnp.arange(TREE_SEGS, dtype=jnp.int32)
    before = (depth[None, :] < depth[:, None]) | (
        (depth[None, :] == depth[:, None]) & (ids[None, :] < ids[:, None])
    )
    rank = jnp.sum(before.astype(jnp.int32), axis=1)
    order = jnp.sum(jnp.where(rank[None, :] == ids[:, None], ids[None, :], 0), axis=1)
    local_heads = columns // HEAD_DIM
    head_ids = plane * local_heads + jnp.arange(local_heads, dtype=jnp.int32)
    own_ids = core * (half // HEAD_DIM) + head_ids
    other_ids = (1 - core) * (half // HEAD_DIM) + head_ids
    slopes = jnp.exp2(-8.0 * (jnp.concatenate([own_ids, other_ids]) + 1).astype(F32) / HEADS)

    tree_unit, _ = normalise(tree.astype(F32))
    normed = (tree_unit * gain_one + shift_one).astype(BF16)
    qkv = (dot_nn(normed, w_heads) + head_shift).astype(BF16)
    mixed = attend(order, slopes, qkv)
    arrived = [mixed[:rows]]
    for k in range(1, planes):
        arrived.append(ring_send(mixed[k * rows : (k + 1) * rows], k))
    attended = jnp.stack(arrived[::-1], axis=0)
    attended = jnp.roll(attended, plane + 1, axis=0)
    attended = attended.reshape(planes, rows, 2, columns).transpose(2, 1, 0, 3)
    attended = attended.reshape(2, rows, half)
    middle = mine.astype(F32) + (
        dot_nn(attended[0], out_own) + dot_nn(attended[1], out_other) + out_shift
    )
    unit_two, scale_two = normalise(middle)
    normed_two = (unit_two * gain_two + shift_two).astype(BF16)
    all_two = jnp.concatenate(gather_rows(normed_two), axis=0)

    def unit(w_up_half, w_down_half, shift):
        pre = dot_nn(all_two, w_up_half) + shift
        below = normal_cdf(pre)
        active = (pre * below).astype(BF16)
        back = dot_nt(all_cot, w_down_half) * (below + pre * normal_pdf(pre))
        return active, back.astype(BF16)

    active_own, back_own = unit(up_own, down_own, up_shift[0:1])
    active_other, back_other = unit(up_other, down_other, up_shift[1:2])

    grad_two = dot_nt(back_own, up_own) + dot_nt(back_other, up_other)
    blocks = [grad_two[k * rows : (k + 1) * rows] for k in range(groups)]
    grad_two = sum_blocks(blocks[0], blocks[1:])
    grad_middle = mine_cot.astype(F32) + norm_back(unit_two, scale_two, gain_two, grad_two)
    grad_branch = grad_middle.astype(BF16)
    grad_mixed = jnp.stack(
        [
            dot_nt(grad_branch, out_own).astype(BF16).reshape(rows, planes, columns),
            dot_nt(grad_branch, out_other).astype(BF16).reshape(rows, planes, columns),
        ],
        axis=1,
    )
    grad_mixed = grad_mixed.transpose(2, 0, 1, 3).reshape(planes, rows, 2 * columns)
    grad_mixed = jnp.roll(grad_mixed, -plane, axis=0)
    back_rows = [grad_mixed[0]]
    for k in range(1, planes):
        back_rows.append(ring_send(grad_mixed[k], k))
    grad_tree = jnp.concatenate(back_rows[:1] + back_rows[:0:-1], axis=0)

    layer_out = dot_nn(active_own, down_own) + dot_nn(active_other, down_other)
    blocks = [layer_out[k * rows : (k + 1) * rows] for k in range(groups)]
    layer_out = middle + (sum_blocks(blocks[0], blocks[1:]) + down_shift)
    layer_out = both_micros(layer_out.astype(BF16))

    grad_down = swap_cores(dot_tn(active_other, all_cot).astype(BF16))
    grad_down = (dot_tn(active_own, all_cot) + grad_down.astype(F32)).astype(BF16)
    grad_down = lax.psum_scatter(grad_down, "context", scatter_dimension=0, tiled=True)
    grad_down = place([piece[None] for piece in exchange(grad_down, 1)], 0)
    grad_up = swap_cores(dot_tn(all_two, back_other).astype(BF16))
    grad_up = (dot_tn(all_two, back_own) + grad_up.astype(F32)).astype(BF16)
    grad_up = grad_up.reshape(groups, planes, part // planes, hidden).transpose(1, 0, 2, 3)
    grad_up = lax.psum_scatter(grad_up, "context", scatter_dimension=0, tiled=True)[0]
    grad_up = exchange(grad_up, 0)
    grad_up = place([piece[0] for piece in grad_up], 1)
    g_down = lax.all_gather(grad_down, "context", axis=1, tiled=False)
    g_up = lax.all_gather(grad_up, "context", axis=0, tiled=True)

    grad_out = swap_cores(dot_tn(attended[1], grad_branch).astype(BF16))
    grad_out = dot_tn(attended[0], grad_branch) + grad_out.astype(F32)
    grad_out = sum_blocks(
        pick(grad_out, 0, 1), [pick(grad_out, k, 1) for k in range(1, groups)]
    )
    g_out = lax.psum(grad_out.astype(BF16), "context")

    grad_qkv = attend_back(order, slopes, qkv, grad_tree)
    grad_normed = dot_nt(grad_qkv, w_heads)
    grad_first = [grad_normed[:rows]]
    for k in range(1, planes):
        sent = grad_normed[k * rows : (k + 1) * rows].astype(BF16)
        grad_first.append(ring_send(sent, k).astype(F32))
    grad_first = sum(grad_first[1:], grad_first[0])
    unit_one, scale_one = normalise(mine.astype(F32))
    grad_tokens = grad_middle + norm_back(unit_one, scale_one, gain_one, grad_first)
    grad_tokens = both_micros(grad_tokens.astype(BF16))

    grad_heads = dot_tn(normed, grad_qkv)
    grad_other = swap_cores(grad_heads[:, 3 * columns :].astype(BF16))
    grad_heads = grad_heads[:, : 3 * columns] + grad_other.astype(F32)
    grad_heads = sum_blocks(
        pick(grad_heads, 0, 0), [pick(grad_heads, k, 0) for k in range(1, groups)]
    ).astype(BF16)
    g_heads = lax.all_gather(grad_heads, "context", axis=0, tiled=False)

    head_sums = jnp.sum(grad_qkv.astype(F32), axis=0).reshape(2, pairs, 3, PAIR)
    head_sums = jnp.stack([head_sums[:, :, 0], head_sums[:, :, 2]], axis=1)
    head_sums = own_first(head_sums.reshape(2, 2, columns)).transpose(1, 0, 2)
    head_row = lax.dynamic_update_slice_in_dim(
        jnp.zeros((2, 2, half), F32), head_sums, plane * columns, 2
    )
    up_sums = own_first(
        jnp.stack([jnp.sum(side.astype(F32), axis=0) for side in (back_own, back_other)])
    )
    up_row = lax.dynamic_update_slice_in_dim(
        jnp.zeros((2, groups * hidden), F32), up_sums, group * hidden, 1
    )
    vectors = jnp.concatenate(
        [
            jnp.sum(grad_normed * tree_unit, axis=0),
            jnp.sum(grad_two * unit_two, axis=0),
            jnp.sum(grad_normed, axis=0),
            jnp.sum(grad_two, axis=0),
            jnp.sum(grad_branch.astype(F32), axis=0),
            jnp.sum(mine_cot.astype(F32), axis=0),
            head_row.reshape(-1),
            up_row.reshape(-1),
        ]
    )
    vectors = lax.psum(vectors, ("fsdp", "context", "tensor")).reshape(-1, width)

    def share(whole):
        return lax.dynamic_slice_in_dim(whole, group * part, part, whole.ndim - 1)

    g_gain = share(vectors[0:2])
    g_shift = share(vectors[2:4])
    g_out_shift = share(vectors[4])
    g_down_shift = share(vectors[5])
    g_qv = lax.dynamic_slice_in_dim(
        vectors[6:8], (core * groups + group) * (part // 2), part // 2, 1
    )
    g_up_shift = lax.dynamic_slice_in_dim(
        vectors[8:].reshape(-1), (core * groups + group) * hidden, hidden, 0
    )
    g_heads = g_heads.reshape(planes, part, pairs, 3, PAIR).transpose(3, 1, 0, 2, 4)
    return (
        layer_out,
        grad_tokens,
        g_gain,
        g_shift,
        g_heads.reshape(3, part, half).astype(F32),
        g_qv,
        g_out.astype(F32),
        g_out_shift,
        g_up.astype(F32),
        g_up_shift,
        g_down.reshape(groups * hidden, part).astype(F32),
        g_down_shift,
    )


def solution(mesh):
    rows = P(None, ("fsdp", "context"), None)
    params = (
        P(None, "fsdp"),
        P(None, "fsdp"),
        P(None, "fsdp", "tensor"),
        P(None, ("tensor", "fsdp")),
        P("tensor", "fsdp"),
        P("fsdp"),
        P("fsdp", "tensor"),
        P(("tensor", "fsdp")),
        P("tensor", "fsdp"),
        P("fsdp"),
    )
    in_specs = (rows, rows, P(None, "fsdp"), P(None, "fsdp")) + params
    return jax.shard_map(
        per_device, mesh=mesh, in_specs=in_specs, out_specs=(rows, rows) + params, check_vma=False
    )
```

```python
from functools import partial

import jax
import jax.numpy as jnp
from jax import lax
from jax.experimental import pallas as pl
from jax.experimental.pallas import tpu as pltpu
from jax.sharding import PartitionSpec as P

HEADS = 32
HEAD_DIM = 64
SEG = 128
TREE_SEGS = 8
LAST_DEPTH = 6
MICRO = 2
PAIR = 2 * HEAD_DIM
NEG_FILL = -1e30
F32 = jnp.float32
BF16 = jnp.bfloat16


def dot_nn(left, right):
    return lax.dot_general(left, right, (((1,), (0,)), ((), ())), preferred_element_type=F32)


def dot_tn(left, right):
    return lax.dot_general(left, right, (((0,), (0,)), ((), ())), preferred_element_type=F32)


def dot_nt(left, right):
    return lax.dot_general(left, right, (((1,), (1,)), ((), ())), preferred_element_type=F32)


def swap_cores(value):
    return lax.ppermute(value, "tensor", [(0, 1), (1, 0)])


def xor_send(value, step):
    size = lax.axis_size("fsdp")
    return lax.ppermute(value, "fsdp", [(i, i ^ step) for i in range(size)])


def ring_send(value, step):
    size = lax.axis_size("context")
    return lax.ppermute(value, "context", [(i, (i + step) % size) for i in range(size)])


def line_step(upward, downward):
    size, step = lax.axis_size("context"), len(upward)
    above = lax.ppermute(upward[-1], "context", [(i, i + 1) for i in range(step - 1, size - 1)])
    below = lax.ppermute(downward[-1], "context", [(i + 1, i) for i in range(0, size - step)])
    return upward + [above], downward + [below]


def line_blocks(upward, downward):
    size, index = lax.axis_size("context"), lax.axis_index("context")
    blocks = [upward[0]]
    for k in range(1, size):
        blocks.append(jnp.where(index + k < size, downward[k], upward[size - k]))
    return blocks


def pass_on(*refs):
    pass


def gate(values, *earlier):
    anywhere = pl.BlockSpec(memory_space=pl.ANY)
    return pl.pallas_call(
        pass_on,
        out_shape=[jax.ShapeDtypeStruct(value.shape, value.dtype) for value in values],
        in_specs=[anywhere] * (len(values) + len(earlier)),
        out_specs=[anywhere] * len(values),
        input_output_aliases={i: i for i in range(len(values))},
        compiler_params=pltpu.CompilerParams(vmem_limit_bytes=1 << 20),
        cost_estimate=pl.CostEstimate(flops=1, transcendentals=0, bytes_accessed=1),
        name="gate",
    )(*values, *earlier)


def zero_from(value):
    first = value[(slice(0, 1),) * value.ndim].reshape(())
    return jnp.minimum(jnp.abs(first.astype(F32)).astype(jnp.int32), 0)


def gather_first(value):
    size = lax.axis_size("fsdp")
    return [xor_send(value, k) for k in ((1, 2) if size == 4 else range(1, size))]


def gather_second(blocks):
    if lax.axis_size("fsdp") != 4:
        return []
    middle = blocks[0].shape[0] // 2
    return [xor_send(blocks[1][:middle], 1), xor_send(blocks[0][middle:], 2)]


def gather_blocks(value, first, second):
    return [value, *first] + ([jnp.concatenate(second, axis=0)] if second else [])


def place(pieces, axis):
    index = lax.axis_index("fsdp")
    width = pieces[0].shape[axis]
    shape = list(pieces[0].shape)
    shape[axis] = width * len(pieces)
    whole = jnp.zeros(shape, pieces[0].dtype)
    for k, piece in enumerate(pieces):
        whole = lax.dynamic_update_slice_in_dim(whole, piece, (index ^ k) * width, axis)
    return whole


def pick(whole, k, axis, offset=0):
    width = whole.shape[axis] // lax.axis_size("fsdp")
    start = (lax.axis_index("fsdp") ^ k) * width + offset
    return lax.dynamic_slice_in_dim(whole, start, width, axis)


def exchange(whole, axis, offset=0):
    blocks = [pick(whole, 0, axis, offset)]
    for k in range(1, lax.axis_size("fsdp")):
        blocks.append(xor_send(pick(whole, k, axis, offset), k))
    return blocks


def send_blocks(pieces):
    return [xor_send(piece, k) for k, piece in enumerate(pieces, 1)]


def add_up(own, pieces):
    return sum([piece.astype(F32) for piece in pieces], own.astype(F32))


def head_lanes(rows):
    return lax.broadcasted_iota(jnp.int32, (rows, PAIR), 1) < HEAD_DIM


def split_heads(value):
    first = head_lanes(value.shape[0])
    zero = jnp.zeros_like(value)
    return jnp.concatenate([jnp.where(first, value, zero), jnp.where(first, zero, value)], axis=0)


def join_heads(stacked):
    first = head_lanes(SEG)
    return jnp.where(first, stacked[:SEG], stacked[SEG:])


def probabilities(stacked_queries, keys, block, slope_a, slope_b):
    width = (block + 1) * SEG
    scores = dot_nt(stacked_queries, keys)
    row = lax.broadcasted_iota(jnp.int32, (2 * SEG, 1), 0)
    column = lax.broadcasted_iota(jnp.int32, (1, width), 1)
    local = jnp.where(row < SEG, row, row - SEG)
    slope = jnp.where(row < SEG, slope_a, slope_b)
    place_row = local + min(block, LAST_DEPTH) * SEG
    place_column = jnp.where(column < (LAST_DEPTH + 1) * SEG, column, column - SEG)
    scores = scores + slope * (place_column - place_row).astype(F32)
    allowed = column <= local + block * SEG
    if block == LAST_DEPTH + 1:
        allowed = allowed & ((column < LAST_DEPTH * SEG) | (column >= (LAST_DEPTH + 1) * SEG))
    scores = jnp.where(allowed, scores, NEG_FILL)
    raised = jnp.exp(scores - jnp.max(scores, axis=-1, keepdims=True))
    return raised * (1.0 / jnp.sum(raised, axis=-1, keepdims=True))


def attention_forward(order, slopes, qkv_ref, out_ref, keys, values):
    pair = pl.program_id(0)
    slope_a, slope_b = slopes[2 * pair], slopes[2 * pair + 1]
    for block in range(TREE_SEGS):
        rows = pl.ds(block * SEG, SEG)
        keys[rows, :] = qkv_ref[order[block], :, PAIR : 2 * PAIR]
        values[rows, :] = qkv_ref[order[block], :, 2 * PAIR : 3 * PAIR]
    for block in range(TREE_SEGS):
        seen = pl.ds(0, (block + 1) * SEG)
        queries = split_heads(qkv_ref[order[block], :, :PAIR] * BF16(HEAD_DIM**-0.5))
        probs = probabilities(queries, keys[seen, :], block, slope_a, slope_b)
        mixed = dot_nn(probs.astype(BF16), values[seen, :])
        out_ref[order[block]] = join_heads(mixed).astype(BF16)


def attention_backward(order, slopes, qkv_ref, grad_ref, out_ref, keys, values, grad_keys, grad_values):
    pair = pl.program_id(0)
    slope_a, slope_b = slopes[2 * pair], slopes[2 * pair + 1]
    for block in range(TREE_SEGS):
        rows = pl.ds(block * SEG, SEG)
        keys[rows, :] = qkv_ref[order[block], :, PAIR : 2 * PAIR]
        values[rows, :] = qkv_ref[order[block], :, 2 * PAIR : 3 * PAIR]
    grad_keys[...] = jnp.zeros_like(grad_keys)
    grad_values[...] = jnp.zeros_like(grad_values)
    for block in range(TREE_SEGS):
        seen = pl.ds(0, (block + 1) * SEG)
        queries = split_heads(qkv_ref[order[block], :, :PAIR] * BF16(HEAD_DIM**-0.5))
        grads = split_heads(grad_ref[order[block]])
        probs = probabilities(queries, keys[seen, :], block, slope_a, slope_b)
        grad_probs = dot_nt(grads, values[seen, :])
        centre = jnp.sum(probs * grad_probs, axis=-1, keepdims=True)
        grad_scores = (probs * (grad_probs - centre)).astype(BF16)
        grad_queries = join_heads(dot_nn(grad_scores, keys[seen, :])) * HEAD_DIM**-0.5
        out_ref[order[block], :, :PAIR] = grad_queries.astype(BF16)
        grad_keys[seen, :] += dot_tn(grad_scores, queries)
        grad_values[seen, :] += dot_tn(probs.astype(BF16), grads)
    for block in range(TREE_SEGS):
        rows = pl.ds(block * SEG, SEG)
        out_ref[order[block], :, PAIR : 2 * PAIR] = grad_keys[rows, :].astype(BF16)
        out_ref[order[block], :, 2 * PAIR : 3 * PAIR] = grad_values[rows, :].astype(BF16)


def block_of(width):
    return pl.BlockSpec((TREE_SEGS, SEG, width), lambda pair, *scalars: (0, 0, pair))


def attend(order, slopes, qkv):
    pairs = qkv.shape[1] // (3 * PAIR)
    rows = TREE_SEGS * SEG
    out = pl.pallas_call(
        attention_forward,
        out_shape=jax.ShapeDtypeStruct((TREE_SEGS, SEG, pairs * PAIR), BF16),
        grid_spec=pltpu.PrefetchScalarGridSpec(
            num_scalar_prefetch=2,
            grid=(pairs,),
            in_specs=[block_of(3 * PAIR)],
            out_specs=block_of(PAIR),
            scratch_shapes=[pltpu.VMEM((rows, PAIR), BF16)] * 2,
        ),
        compiler_params=pltpu.CompilerParams(vmem_limit_bytes=48 << 20),
        cost_estimate=pl.CostEstimate(
            flops=pairs * 32 * rows * rows * PAIR, transcendentals=0, bytes_accessed=1
        ),
        name="attend",
    )(order, slopes, qkv.reshape(TREE_SEGS, SEG, -1))
    return out.reshape(rows, pairs * PAIR)


def attend_back(order, slopes, qkv, grad):
    pairs = qkv.shape[1] // (3 * PAIR)
    rows = TREE_SEGS * SEG
    out = pl.pallas_call(
        attention_backward,
        out_shape=jax.ShapeDtypeStruct((TREE_SEGS, SEG, pairs * 3 * PAIR), BF16),
        grid_spec=pltpu.PrefetchScalarGridSpec(
            num_scalar_prefetch=2,
            grid=(pairs,),
            in_specs=[block_of(3 * PAIR), block_of(PAIR)],
            out_specs=block_of(3 * PAIR),
            scratch_shapes=[pltpu.VMEM((rows, PAIR), BF16)] * 2 + [pltpu.VMEM((rows, PAIR), F32)] * 2,
        ),
        compiler_params=pltpu.CompilerParams(vmem_limit_bytes=48 << 20),
        cost_estimate=pl.CostEstimate(
            flops=pairs * 60 * rows * rows * PAIR, transcendentals=0, bytes_accessed=1
        ),
        name="attend_back",
    )(order, slopes, qkv.reshape(TREE_SEGS, SEG, -1), grad.reshape(TREE_SEGS, SEG, -1))
    return out.reshape(rows, pairs * 3 * PAIR)


def normalise(rows):
    centred = rows - jnp.mean(rows, axis=-1, keepdims=True)
    scale = lax.rsqrt(jnp.mean(centred * centred, axis=-1, keepdims=True) + 1e-05)
    return centred * scale, scale


def norm_back(unit, scale, gain, upstream):
    weighted = upstream * gain
    centre = jnp.mean(weighted, axis=-1, keepdims=True)
    along = jnp.mean(weighted * unit, axis=-1, keepdims=True)
    return scale * (weighted - centre - unit * along)


def normal_cdf(value):
    return 0.5 * (1.0 + lax.erf(value * 0.7071067811865476))


def normal_pdf(value):
    return 0.3989422804014327 * jnp.exp(-0.5 * value * value)


def both_micros(mine):
    other = swap_cores(mine)
    first = lax.axis_index("tensor") == 0
    return jnp.stack([jnp.where(first, mine, other), jnp.where(first, other, mine)])


def per_device(
    tokens,
    cotangent,
    seg_parent,
    positions,
    norm_gain,
    norm_bias,
    w_qkv,
    bias_qv,
    w_out,
    bias_out,
    w_up,
    bias_up,
    w_down,
    bias_down,
):
    planes, groups = lax.axis_size("context"), lax.axis_size("fsdp")
    plane, group, core = (lax.axis_index(name) for name in ("context", "fsdp", "tensor"))
    rows, width = tokens.shape[1], tokens.shape[2]
    part = width // groups
    half = w_qkv.shape[2]
    columns = half // planes
    pairs = columns // PAIR
    hidden = w_up.shape[1] // groups

    def rows_of(whole, k):
        return lax.dynamic_slice_in_dim(whole, ((plane + k) % planes) * rows, rows, 0)

    mine = lax.dynamic_index_in_dim(tokens, core, 0, keepdims=False)
    mine_cot = lax.dynamic_index_in_dim(cotangent, core, 0, keepdims=False)
    packed = jnp.concatenate(
        [
            norm_gain,
            norm_bias,
            bias_out[None],
            bias_down[None],
            bias_qv.reshape(1, part),
            bias_up.reshape(-1, part),
        ],
        axis=0,
    )
    lines = packed.size // (3 * columns)
    chosen = lax.dynamic_slice_in_dim(w_qkv, plane * columns, columns, 2)
    chosen = chosen.reshape(3, part, pairs, PAIR).transpose(1, 2, 0, 3).reshape(part, 3 * columns)
    chosen = jnp.concatenate(
        [
            chosen,
            packed.reshape(lines, 3 * columns),
            jnp.zeros((-lines % 32, 3 * columns), BF16),
        ],
        axis=0,
    )
    up_pieces = [pick(w_up, k, 1) for k in range(groups)]
    down_rows = lax.dynamic_index_in_dim(
        w_down.reshape(groups, planes, hidden // planes, part), plane, 1, keepdims=False
    )
    down_pieces = [pick(down_rows, k, 0)[0] for k in range(groups)]

    tree = lax.all_gather(mine, "context", axis=0, tiled=True)
    head_first = gather_first(chosen)
    rest = gate([*head_first, *up_pieces[1:]])
    head_first, up_pieces[1:] = rest[: len(head_first)], rest[len(head_first) :]
    head_second = gather_second(head_first)
    up_blocks = up_pieces[:1] + send_blocks(up_pieces[1:])
    tree, mine_cot, *down_pieces = gate([tree, mine_cot, *down_pieces], *head_second)
    head_blocks = gather_blocks(chosen, head_first, head_second)
    heads_own = place([block[:part] for block in head_blocks], 0)
    w_heads = jnp.concatenate([heads_own, swap_cores(heads_own)], axis=1)

    small = [block[part : part + lines].reshape(1, -1, part) for block in head_blocks]
    small = place(small, 0)
    small = jnp.stack([small, swap_cores(small)])
    spread = small[0, :, :6].astype(F32).transpose(1, 0, 2).reshape(6, width)
    gain_one, gain_two, shift_one, shift_two, out_shift, down_shift = (
        spread[i : i + 1] for i in range(6)
    )
    head_shift = small[:, :, 6].astype(F32).reshape(2, groups, 2, part // 2).transpose(0, 2, 1, 3)
    head_shift = lax.dynamic_slice_in_dim(
        head_shift.reshape(2, 2, half), plane * columns, columns, 2
    ).reshape(2, 2, pairs, PAIR)
    head_shift = jnp.stack(
        [head_shift[:, 0], jnp.zeros_like(head_shift[:, 0]), head_shift[:, 1]], axis=2
    ).reshape(1, 2 * pairs * 3 * PAIR)
    up_shift = lax.dynamic_index_in_dim(small, group, 1, keepdims=False)[:, 7:]
    up_shift = up_shift.astype(F32).reshape(2, hidden)

    depth = lax.dynamic_index_in_dim(positions, core, 0, keepdims=False)[::SEG] // SEG
    ids = jnp.arange(TREE_SEGS, dtype=jnp.int32)
    before = (depth[None, :] < depth[:, None]) | (
        (depth[None, :] == depth[:, None]) & (ids[None, :] < ids[:, None])
    )
    rank = jnp.sum(before.astype(jnp.int32), axis=1)
    order = jnp.sum(jnp.where(rank[None, :] == ids[:, None], ids[None, :], 0), axis=1)
    local_heads = columns // HEAD_DIM
    head_ids = plane * local_heads + jnp.arange(local_heads, dtype=jnp.int32)
    own_ids = core * (half // HEAD_DIM) + head_ids
    other_ids = (1 - core) * (half // HEAD_DIM) + head_ids
    slopes = jnp.exp2(-8.0 * (jnp.concatenate([own_ids, other_ids]) + 1).astype(F32) / HEADS)

    mine_out = lax.dynamic_slice_in_dim(w_out, zero_from(mine_cot), half, 0)
    out_first = gather_first(mine_out)
    tree_unit, _ = normalise(tree.astype(F32))
    normed = (tree_unit * gain_one + shift_one).astype(BF16)
    qkv = (dot_nn(normed, w_heads) + head_shift).astype(BF16)
    qkv, *rest = gate([qkv, *out_first, *down_pieces[1:]], *up_blocks[1:])
    out_first, down_pieces[1:] = rest[: len(out_first)], rest[len(out_first) :]
    out_second = gather_second(out_first)
    down_blocks = down_pieces[:1] + send_blocks(down_pieces[1:])
    mixed = attend(order, slopes, qkv)
    mixed, mine_cot, *down_blocks = gate([mixed, mine_cot, *down_blocks], *out_second)
    out_own = place(gather_blocks(mine_out, out_first, out_second), 1)
    down_rows = place(down_blocks, 1)
    up_own = place(up_blocks, 0)
    up_other, out_other = swap_cores(up_own), swap_cores(out_own)

    arrived = [rows_of(mixed, 0)]
    for k in range(1, planes):
        arrived.append(ring_send(rows_of(mixed, k), k))
    cot_first = gather_first(mine_cot)
    out_other, *rest = gate([out_other, *arrived, *cot_first])
    arrived, cot_first = rest[:planes], rest[planes:]
    down_own = lax.all_gather(down_rows, "context", axis=0, tiled=True)
    cot_second = gather_second(cot_first)
    attended = jnp.stack(arrived[::-1], axis=0)
    attended = jnp.roll(attended, plane + 1, axis=0)
    attended = attended.reshape(planes, rows, 2, columns).transpose(2, 1, 0, 3)
    attended = attended.reshape(2, rows, half)
    middle = mine.astype(F32) + (
        dot_nn(attended[0], out_own) + dot_nn(attended[1], out_other) + out_shift
    )
    unit_two, scale_two = normalise(middle)
    normed_two = (unit_two * gain_two + shift_two).astype(BF16)
    (normed_two,) = gate([normed_two], *cot_second)
    two_first = gate(gather_first(normed_two))
    two_second = gather_second(two_first)
    all_two = jnp.concatenate(gather_blocks(normed_two, two_first, two_second), axis=0)
    all_cot = jnp.concatenate(gather_blocks(mine_cot, cot_first, cot_second), axis=0)

    pre_other = dot_nn(all_two, up_other) + up_shift[1:2]
    active_other = (pre_other * normal_cdf(pre_other)).astype(BF16)
    grad_down = swap_cores(dot_tn(active_other, all_cot).astype(BF16))
    pre_own = dot_nn(all_two, up_own) + up_shift[0:1]
    active_own = (pre_own * normal_cdf(pre_own)).astype(BF16)
    grad_down = (dot_tn(active_own, all_cot) + grad_down.astype(F32)).astype(BF16)

    def slope_of(pre):
        return normal_cdf(pre) + pre * normal_pdf(pre)

    (down_own,) = gate([down_own], grad_down)
    down_other = swap_cores(down_own)
    back_other = (dot_nt(all_cot, down_other) * slope_of(pre_other)).astype(BF16)
    back_own = (dot_nt(all_cot, down_own) * slope_of(pre_own)).astype(BF16)

    grad_two = (dot_nt(back_own, up_own) + dot_nt(back_other, up_other)).astype(BF16)
    back_other_in = back_other
    back_other, own_two, *sent = gate(
        [back_other] + [grad_two[k * rows : (k + 1) * rows] for k in range(groups)]
    )
    grad_down = lax.psum_scatter(grad_down, "context", scatter_dimension=0, tiled=True)
    grad_two = send_blocks(sent)
    grad_up = swap_cores(dot_tn(all_two, back_other).astype(BF16))
    grad_up = (dot_tn(all_two, back_own) + grad_up.astype(F32)).astype(BF16)
    grad_up = grad_up.reshape(groups, planes, part // planes, hidden).transpose(1, 0, 2, 3)
    grad_up = grad_up.reshape(width, hidden)
    grad_down, *grad_two = gate([grad_down, *grad_two], grad_up)
    grad_up = lax.psum_scatter(grad_up, "context", scatter_dimension=0, tiled=True)

    grad_two = add_up(own_two, grad_two)
    grad_middle = mine_cot.astype(F32) + norm_back(unit_two, scale_two, gain_two, grad_two)
    grad_branch = grad_middle.astype(BF16)
    grad_mixed = jnp.stack(
        [
            dot_nt(grad_branch, out_own).astype(BF16).reshape(rows, planes, columns),
            dot_nt(grad_branch, out_other).astype(BF16).reshape(rows, planes, columns),
        ],
        axis=1,
    )
    grad_mixed = grad_mixed.transpose(2, 0, 1, 3).reshape(planes, rows, 2 * columns)
    grad_mixed = jnp.roll(grad_mixed, -plane, axis=0)
    grad_down = exchange(grad_down, 1)
    grad_mixed = gate([grad_mixed[k] for k in range(planes)])

    back_rows = [grad_mixed[0]]
    for k in range(1, planes):
        back_rows.append(ring_send(grad_mixed[k], k))
    grad_out = swap_cores(dot_tn(attended[1], grad_branch).astype(BF16))
    grad_out = dot_tn(attended[0], grad_branch) + grad_out.astype(F32)
    grad_tree = jnp.roll(jnp.stack(back_rows[:1] + back_rows[:0:-1]), plane, axis=0)
    grad_tree = grad_tree.reshape(planes * rows, 2 * columns)
    out_blocks = [pick(grad_out, k, 1) for k in range(groups)]
    out_own_block, out_blocks = out_blocks[0], [piece.astype(BF16) for piece in out_blocks[1:]]
    grad_tree, grad_up, *grad_down = gate([grad_tree, grad_up, *grad_down])
    grad_down = place([piece[None] for piece in grad_down], 0)

    down_up, down_down = line_step([grad_down], [grad_down])
    grad_up = exchange(grad_up.reshape(groups, part // planes, hidden), 0)
    grad_qkv = attend_back(order, slopes, qkv, grad_tree)
    grad_qkv, down_up[-1], down_down[-1], *rest = gate(
        [grad_qkv, down_up[-1], down_down[-1], *grad_up, *out_blocks]
    )
    grad_up, out_blocks = rest[:groups], rest[groups:]

    grad_up = place([piece[0] for piece in grad_up], 1)
    grad_normed = dot_nt(grad_qkv, w_heads)
    head_sums = jnp.sum(grad_qkv.astype(F32), axis=0).reshape(2, pairs, 3, PAIR)
    head_sums = jnp.stack([head_sums[:, :, 0], head_sums[:, :, 2]], axis=1)
    head_row = lax.dynamic_update_slice_in_dim(
        jnp.zeros((2, 2, half), F32), head_sums.reshape(2, 2, columns), plane * columns, 2
    )
    up_sums = [jnp.sum(side.astype(F32), axis=0) for side in (back_own, back_other_in)]
    sums = jnp.concatenate(
        [
            jnp.sum(grad_normed * tree_unit, axis=0),
            jnp.sum(grad_two * unit_two, axis=0),
            jnp.sum(grad_normed, axis=0),
            jnp.sum(grad_two, axis=0),
            jnp.sum(grad_branch.astype(F32), axis=0),
            jnp.sum(mine_cot.astype(F32), axis=0),
            head_row.reshape(-1),
            *up_sums,
        ]
    )
    lines = -(-sums.shape[0] // (16 * width)) * 16
    sums = jnp.pad(sums, (0, lines * width - sums.shape[0])).reshape(lines, width)
    blocks = [
        jnp.concatenate([grad_normed[k * rows : (k + 1) * rows], sums]) for k in range(planes)
    ]
    blocks = jnp.concatenate(blocks).astype(BF16)
    blocks, grad_qkv, down_up[-1], down_down[-1], *out_blocks = gate(
        [blocks, grad_qkv, down_up[-1], down_down[-1], *out_blocks]
    )
    later = zero_from(blocks)
    grad_first = lax.psum_scatter(blocks, "context", scatter_dimension=0, tiled=True)
    g_up = lax.all_gather(grad_up, "context", axis=0, tiled=True)

    down_up, down_down = line_step(down_up, down_down)
    grad_heads = dot_tn(normed, grad_qkv)
    head_other = swap_cores(grad_heads[:, 3 * columns :].astype(BF16))
    grad_heads = grad_heads[:, : 3 * columns] + head_other.astype(F32)
    head_pieces = [pick(grad_heads, k, 0).astype(BF16) for k in range(1, groups)]
    grad_heads = add_up(pick(grad_heads, 0, 0), send_blocks(head_pieces)).astype(BF16)
    grad_heads = grad_heads.reshape(part, pairs, 3, PAIR).transpose(2, 0, 1, 3)
    grad_heads = grad_heads.reshape(3 * part, columns)
    out_blocks = send_blocks(out_blocks)
    layer_out = dot_nn(
        lax.dynamic_slice_in_dim(active_own, later, groups * rows, 0), down_own
    ) + dot_nn(lax.dynamic_slice_in_dim(active_other, later, groups * rows, 0), down_other)
    layer_out = layer_out.astype(BF16)
    grad_first, grad_heads, down_up[-1], down_down[-1], out_own_block, *layer_blocks = gate(
        [grad_first, grad_heads, down_up[-1], down_down[-1], out_own_block]
        + [layer_out[k * rows : (k + 1) * rows] for k in range(groups)],
        *out_blocks,
        g_up,
    )
    while len(down_up) < planes:
        down_up, down_down = line_step(down_up, down_down)
    grad_out = add_up(out_own_block, out_blocks).astype(BF16)
    grad_out = lax.psum_scatter(grad_out, "context", scatter_dimension=0, tiled=True)
    layer_out = add_up(layer_blocks[0], send_blocks(layer_blocks[1:]))
    layer_out = middle + (layer_out + down_shift)
    layer_out = both_micros(layer_out.astype(BF16))
    grad_heads, grad_out = gate([grad_heads, grad_out], down_up[-1], down_down[-1])

    lines = grad_out.shape[0]
    last = [grad_heads] + [
        grad_out[:, i : i + columns] for i in range(0, part, columns)
    ]
    last = lax.all_gather(jnp.concatenate(last), "context", axis=1, tiled=True)
    g_heads = last[: 3 * part]
    g_out = last[3 * part :].reshape(part // columns, lines, planes, columns)
    g_out = g_out.transpose(2, 1, 0, 3).reshape(half, part)
    g_down = jnp.zeros((groups, planes, hidden // planes, part), F32)
    for k, piece in enumerate(line_blocks(down_up, down_down)):
        g_down = lax.dynamic_update_slice_in_dim(
            g_down, piece.astype(F32)[:, None], (plane + k) % planes, 1
        )

    sums = grad_first[rows:].astype(F32).reshape(-1)
    grad_first = grad_first[:rows].astype(F32)
    unit_one, scale_one = normalise(mine.astype(F32))
    grad_tokens = grad_middle + norm_back(unit_one, scale_one, gain_one, grad_first)
    grad_tokens = both_micros(grad_tokens.astype(BF16))

    spread = sums[: 6 * width].reshape(6, groups, part)
    spread = spread.transpose(1, 0, 2).reshape(groups, 6 * part)
    head_row = sums[6 * width : 8 * width].reshape(4, groups, part // 2)
    head_row = head_row.transpose(1, 0, 2).reshape(groups, 2 * part)
    up_sums = sums[8 * width : 8 * width + 2 * hidden].reshape(2, hidden)
    sums = jnp.concatenate([spread, head_row], axis=1)
    total = pick(sums, 0, 0)
    for k in range(1, groups):
        total = total + xor_send(pick(sums, k, 0), k)
    total = total[0]
    total_other = swap_cores(jnp.concatenate([total[: 6 * part], total[7 * part :], up_sums[1]]))
    total = jnp.concatenate([total[: 7 * part], up_sums[0]]) + total_other
    wide = total[: 6 * part].reshape(6, part)
    return (
        layer_out,
        grad_tokens,
        wide[0:2],
        wide[2:4],
        g_heads.astype(F32).reshape(3, part, half),
        total[6 * part : 7 * part].reshape(2, part // 2),
        g_out.astype(F32),
        wide[4],
        g_up.astype(F32),
        total[7 * part :],
        g_down.reshape(groups * hidden, part),
        wide[5],
    )


def solution(mesh):
    rows = P(None, ("fsdp", "context"), None)
    params = (
        P(None, "fsdp"),
        P(None, "fsdp"),
        P(None, "fsdp", "tensor"),
        P(None, ("tensor", "fsdp")),
        P("tensor", "fsdp"),
        P("fsdp"),
        P("fsdp", "tensor"),
        P(("tensor", "fsdp")),
        P("tensor", "fsdp"),
        P("fsdp"),
    )
    in_specs = (rows, rows, P(None, "fsdp"), P(None, "fsdp")) + params
    return jax.shard_map(
        per_device, mesh=mesh, in_specs=in_specs, out_specs=(rows, rows) + params, check_vma=False
    )
```

```python
from functools import partial

import jax
import jax.numpy as jnp
from jax import lax
from jax.experimental import pallas as pl
from jax.experimental.pallas import tpu as pltpu
from jax.sharding import PartitionSpec as P

HEADS = 32
HEAD_DIM = 64
SEG = 128
TREE_SEGS = 8
LAST_DEPTH = 6
MICRO = 2
PAIR = 2 * HEAD_DIM
NEG_FILL = -1e30
F32 = jnp.float32
BF16 = jnp.bfloat16


def dot_nn(left, right):
    return lax.dot_general(left, right, (((1,), (0,)), ((), ())), preferred_element_type=F32)


def dot_tn(left, right):
    return lax.dot_general(left, right, (((0,), (0,)), ((), ())), preferred_element_type=F32)


def dot_nt(left, right):
    return lax.dot_general(left, right, (((1,), (1,)), ((), ())), preferred_element_type=F32)


def swap_cores(value):
    return lax.ppermute(value, "tensor", [(0, 1), (1, 0)])


def xor_send(value, step):
    size = lax.axis_size("fsdp")
    return lax.ppermute(value, "fsdp", [(i, i ^ step) for i in range(size)])


def ring_send(value, step):
    size = lax.axis_size("context")
    return lax.ppermute(value, "context", [(i, (i + step) % size) for i in range(size)])


def line_step(upward, downward):
    size, step = lax.axis_size("context"), len(upward)
    above = lax.ppermute(upward[-1], "context", [(i, i + 1) for i in range(step - 1, size - 1)])
    below = lax.ppermute(downward[-1], "context", [(i + 1, i) for i in range(0, size - step)])
    return upward + [above], downward + [below]


def line_blocks(upward, downward):
    size, index = lax.axis_size("context"), lax.axis_index("context")
    blocks = [upward[0]]
    for k in range(1, size):
        blocks.append(jnp.where(index + k < size, downward[k], upward[size - k]))
    return blocks


def pass_on(*refs):
    pass


def gate(values, *earlier):
    anywhere = pl.BlockSpec(memory_space=pl.ANY)
    return pl.pallas_call(
        pass_on,
        out_shape=[jax.ShapeDtypeStruct(value.shape, value.dtype) for value in values],
        in_specs=[anywhere] * (len(values) + len(earlier)),
        out_specs=[anywhere] * len(values),
        input_output_aliases={i: i for i in range(len(values))},
        compiler_params=pltpu.CompilerParams(vmem_limit_bytes=1 << 20),
        cost_estimate=pl.CostEstimate(flops=1, transcendentals=0, bytes_accessed=1),
        name="gate",
    )(*values, *earlier)


def zero_from(value):
    first = value[(slice(0, 1),) * value.ndim].reshape(())
    return jnp.minimum(jnp.abs(first.astype(F32)).astype(jnp.int32), 0)


def gather_first(value):
    size = lax.axis_size("fsdp")
    return [xor_send(value, k) for k in ((1, 2) if size == 4 else range(1, size))]


def gather_second(blocks):
    if lax.axis_size("fsdp") != 4:
        return []
    middle = blocks[0].shape[0] // 2
    return [xor_send(blocks[1][:middle], 1), xor_send(blocks[0][middle:], 2)]


def gather_blocks(value, first, second):
    return [value, *first] + ([jnp.concatenate(second, axis=0)] if second else [])


def place(pieces, axis):
    index = lax.axis_index("fsdp")
    width = pieces[0].shape[axis]
    shape = list(pieces[0].shape)
    shape[axis] = width * len(pieces)
    whole = jnp.zeros(shape, pieces[0].dtype)
    for k, piece in enumerate(pieces):
        whole = lax.dynamic_update_slice_in_dim(whole, piece, (index ^ k) * width, axis)
    return whole


def pick(whole, k, axis, offset=0):
    width = whole.shape[axis] // lax.axis_size("fsdp")
    start = (lax.axis_index("fsdp") ^ k) * width + offset
    return lax.dynamic_slice_in_dim(whole, start, width, axis)


def exchange(whole, axis, offset=0):
    blocks = [pick(whole, 0, axis, offset)]
    for k in range(1, lax.axis_size("fsdp")):
        blocks.append(xor_send(pick(whole, k, axis, offset), k))
    return blocks


def send_blocks(pieces):
    return [xor_send(piece, k) for k, piece in enumerate(pieces, 1)]


def add_up(own, pieces):
    return sum([piece.astype(F32) for piece in pieces], own.astype(F32))


def head_lanes(rows):
    return lax.broadcasted_iota(jnp.int32, (rows, PAIR), 1) < HEAD_DIM


def split_heads(value):
    first = head_lanes(value.shape[0])
    zero = jnp.zeros_like(value)
    return jnp.concatenate([jnp.where(first, value, zero), jnp.where(first, zero, value)], axis=0)


def join_heads(stacked):
    first = head_lanes(SEG)
    return jnp.where(first, stacked[:SEG], stacked[SEG:])


def probabilities(stacked_queries, keys, block, slope_a, slope_b):
    width = (block + 1) * SEG
    scores = dot_nt(stacked_queries, keys)
    row = lax.broadcasted_iota(jnp.int32, (2 * SEG, 1), 0)
    column = lax.broadcasted_iota(jnp.int32, (1, width), 1)
    local = jnp.where(row < SEG, row, row - SEG)
    slope = jnp.where(row < SEG, slope_a, slope_b)
    place_row = local + min(block, LAST_DEPTH) * SEG
    place_column = jnp.where(column < (LAST_DEPTH + 1) * SEG, column, column - SEG)
    scores = scores + slope * (place_column - place_row).astype(F32)
    allowed = column <= local + block * SEG
    if block == LAST_DEPTH + 1:
        allowed = allowed & ((column < LAST_DEPTH * SEG) | (column >= (LAST_DEPTH + 1) * SEG))
    scores = jnp.where(allowed, scores, NEG_FILL)
    raised = jnp.exp(scores - jnp.max(scores, axis=-1, keepdims=True))
    return raised * (1.0 / jnp.sum(raised, axis=-1, keepdims=True))


def attention_forward(order, slopes, qkv_ref, out_ref, keys, values):
    pair = pl.program_id(0)
    slope_a, slope_b = slopes[2 * pair], slopes[2 * pair + 1]
    for block in range(TREE_SEGS):
        rows = pl.ds(block * SEG, SEG)
        keys[rows, :] = qkv_ref[order[block], :, PAIR : 2 * PAIR]
        values[rows, :] = qkv_ref[order[block], :, 2 * PAIR : 3 * PAIR]
    for block in range(TREE_SEGS):
        seen = pl.ds(0, (block + 1) * SEG)
        queries = split_heads(qkv_ref[order[block], :, :PAIR] * BF16(HEAD_DIM**-0.5))
        probs = probabilities(queries, keys[seen, :], block, slope_a, slope_b)
        mixed = dot_nn(probs.astype(BF16), values[seen, :])
        out_ref[order[block]] = join_heads(mixed).astype(BF16)


def attention_backward(order, slopes, qkv_ref, grad_ref, out_ref, keys, values, grad_keys, grad_values):
    pair = pl.program_id(0)
    slope_a, slope_b = slopes[2 * pair], slopes[2 * pair + 1]
    for block in range(TREE_SEGS):
        rows = pl.ds(block * SEG, SEG)
        keys[rows, :] = qkv_ref[order[block], :, PAIR : 2 * PAIR]
        values[rows, :] = qkv_ref[order[block], :, 2 * PAIR : 3 * PAIR]
    grad_keys[...] = jnp.zeros_like(grad_keys)
    grad_values[...] = jnp.zeros_like(grad_values)
    for block in range(TREE_SEGS):
        seen = pl.ds(0, (block + 1) * SEG)
        queries = split_heads(qkv_ref[order[block], :, :PAIR] * BF16(HEAD_DIM**-0.5))
        grads = split_heads(grad_ref[order[block]])
        probs = probabilities(queries, keys[seen, :], block, slope_a, slope_b)
        grad_probs = dot_nt(grads, values[seen, :])
        centre = jnp.sum(probs * grad_probs, axis=-1, keepdims=True)
        grad_scores = (probs * (grad_probs - centre)).astype(BF16)
        grad_queries = join_heads(dot_nn(grad_scores, keys[seen, :])) * HEAD_DIM**-0.5
        out_ref[order[block], :, :PAIR] = grad_queries.astype(BF16)
        grad_keys[seen, :] += dot_tn(grad_scores, queries)
        grad_values[seen, :] += dot_tn(probs.astype(BF16), grads)
    for block in range(TREE_SEGS):
        rows = pl.ds(block * SEG, SEG)
        out_ref[order[block], :, PAIR : 2 * PAIR] = grad_keys[rows, :].astype(BF16)
        out_ref[order[block], :, 2 * PAIR : 3 * PAIR] = grad_values[rows, :].astype(BF16)


def block_of(width):
    return pl.BlockSpec((TREE_SEGS, SEG, width), lambda pair, *scalars: (0, 0, pair))


def attend(order, slopes, qkv):
    pairs = qkv.shape[1] // (3 * PAIR)
    rows = TREE_SEGS * SEG
    out = pl.pallas_call(
        attention_forward,
        out_shape=jax.ShapeDtypeStruct((TREE_SEGS, SEG, pairs * PAIR), BF16),
        grid_spec=pltpu.PrefetchScalarGridSpec(
            num_scalar_prefetch=2,
            grid=(pairs,),
            in_specs=[block_of(3 * PAIR)],
            out_specs=block_of(PAIR),
            scratch_shapes=[pltpu.VMEM((rows, PAIR), BF16)] * 2,
        ),
        compiler_params=pltpu.CompilerParams(vmem_limit_bytes=48 << 20),
        cost_estimate=pl.CostEstimate(
            flops=pairs * 32 * rows * rows * PAIR, transcendentals=0, bytes_accessed=1
        ),
        name="attend",
    )(order, slopes, qkv.reshape(TREE_SEGS, SEG, -1))
    return out.reshape(rows, pairs * PAIR)


def attend_back(order, slopes, qkv, grad):
    pairs = qkv.shape[1] // (3 * PAIR)
    rows = TREE_SEGS * SEG
    out = pl.pallas_call(
        attention_backward,
        out_shape=jax.ShapeDtypeStruct((TREE_SEGS, SEG, pairs * 3 * PAIR), BF16),
        grid_spec=pltpu.PrefetchScalarGridSpec(
            num_scalar_prefetch=2,
            grid=(pairs,),
            in_specs=[block_of(3 * PAIR), block_of(PAIR)],
            out_specs=block_of(3 * PAIR),
            scratch_shapes=[pltpu.VMEM((rows, PAIR), BF16)] * 2 + [pltpu.VMEM((rows, PAIR), F32)] * 2,
        ),
        compiler_params=pltpu.CompilerParams(vmem_limit_bytes=48 << 20),
        cost_estimate=pl.CostEstimate(
            flops=pairs * 60 * rows * rows * PAIR, transcendentals=0, bytes_accessed=1
        ),
        name="attend_back",
    )(order, slopes, qkv.reshape(TREE_SEGS, SEG, -1), grad.reshape(TREE_SEGS, SEG, -1))
    return out.reshape(rows, pairs * 3 * PAIR)


def normalise(rows):
    centred = rows - jnp.mean(rows, axis=-1, keepdims=True)
    scale = lax.rsqrt(jnp.mean(centred * centred, axis=-1, keepdims=True) + 1e-05)
    return centred * scale, scale


def norm_back(unit, scale, gain, upstream):
    weighted = upstream * gain
    centre = jnp.mean(weighted, axis=-1, keepdims=True)
    along = jnp.mean(weighted * unit, axis=-1, keepdims=True)
    return scale * (weighted - centre - unit * along)


def normal_cdf(value):
    return 0.5 * (1.0 + lax.erf(value * 0.7071067811865476))


def normal_pdf(value):
    return 0.3989422804014327 * jnp.exp(-0.5 * value * value)


def both_micros(mine):
    other = swap_cores(mine)
    first = lax.axis_index("tensor") == 0
    return jnp.stack([jnp.where(first, mine, other), jnp.where(first, other, mine)])


def per_device(
    tokens,
    cotangent,
    seg_parent,
    positions,
    norm_gain,
    norm_bias,
    w_qkv,
    bias_qv,
    w_out,
    bias_out,
    w_up,
    bias_up,
    w_down,
    bias_down,
):
    planes, groups = lax.axis_size("context"), lax.axis_size("fsdp")
    plane, group, core = (lax.axis_index(name) for name in ("context", "fsdp", "tensor"))
    rows, width = tokens.shape[1], tokens.shape[2]
    part = width // groups
    half = w_qkv.shape[2]
    columns = half // planes
    pairs = columns // PAIR
    hidden = w_up.shape[1] // groups

    def rows_of(whole, k):
        return lax.dynamic_slice_in_dim(whole, ((plane + k) % planes) * rows, rows, 0)

    mine = lax.dynamic_index_in_dim(tokens, core, 0, keepdims=False)
    mine_cot = lax.dynamic_index_in_dim(cotangent, core, 0, keepdims=False)
    packed = jnp.concatenate(
        [
            norm_gain,
            norm_bias,
            bias_out[None],
            bias_down[None],
            bias_qv.reshape(1, part),
            bias_up.reshape(-1, part),
        ],
        axis=0,
    )
    lines = packed.size // (3 * columns)
    chosen = lax.dynamic_slice_in_dim(w_qkv, plane * columns, columns, 2)
    chosen = chosen.reshape(3, part, pairs, PAIR).transpose(1, 2, 0, 3).reshape(part, 3 * columns)
    chosen = jnp.concatenate(
        [
            chosen,
            packed.reshape(lines, 3 * columns),
            jnp.zeros((-lines % 32, 3 * columns), BF16),
        ],
        axis=0,
    )
    up_pieces = [pick(w_up, k, 1) for k in range(groups)]
    down_pieces = [pick(w_down, k, 0) for k in range(groups)]

    tree = lax.all_gather(mine, "context", axis=0, tiled=True)
    head_first = gather_first(chosen)
    rest = gate([*head_first, *up_pieces[1:]])
    head_first, up_pieces[1:] = rest[: len(head_first)], rest[len(head_first) :]
    head_second = gather_second(head_first)
    up_blocks = up_pieces[:1] + send_blocks(up_pieces[1:])
    tree, mine_cot, *down_pieces = gate([tree, mine_cot, *down_pieces], *head_second)
    head_blocks = gather_blocks(chosen, head_first, head_second)
    heads_own = place([block[:part] for block in head_blocks], 0)
    w_heads = jnp.concatenate([heads_own, swap_cores(heads_own)], axis=1)

    small = [block[part : part + lines].reshape(1, -1, part) for block in head_blocks]
    small = place(small, 0)
    small = jnp.stack([small, swap_cores(small)])
    spread = small[0, :, :6].astype(F32).transpose(1, 0, 2).reshape(6, width)
    gain_one, gain_two, shift_one, shift_two, out_shift, down_shift = (
        spread[i : i + 1] for i in range(6)
    )
    head_shift = small[:, :, 6].astype(F32).reshape(2, groups, 2, part // 2).transpose(0, 2, 1, 3)
    head_shift = lax.dynamic_slice_in_dim(
        head_shift.reshape(2, 2, half), plane * columns, columns, 2
    ).reshape(2, 2, pairs, PAIR)
    head_shift = jnp.stack(
        [head_shift[:, 0], jnp.zeros_like(head_shift[:, 0]), head_shift[:, 1]], axis=2
    ).reshape(1, 2 * pairs * 3 * PAIR)
    up_shift = lax.dynamic_index_in_dim(small, group, 1, keepdims=False)[:, 7:]
    up_shift = up_shift.astype(F32).reshape(2, hidden)

    depth = lax.dynamic_index_in_dim(positions, core, 0, keepdims=False)[::SEG] // SEG
    ids = jnp.arange(TREE_SEGS, dtype=jnp.int32)
    before = (depth[None, :] < depth[:, None]) | (
        (depth[None, :] == depth[:, None]) & (ids[None, :] < ids[:, None])
    )
    rank = jnp.sum(before.astype(jnp.int32), axis=1)
    order = jnp.sum(jnp.where(rank[None, :] == ids[:, None], ids[None, :], 0), axis=1)
    local_heads = columns // HEAD_DIM
    head_ids = plane * local_heads + jnp.arange(local_heads, dtype=jnp.int32)
    own_ids = core * (half // HEAD_DIM) + head_ids
    other_ids = (1 - core) * (half // HEAD_DIM) + head_ids
    slopes = jnp.exp2(-8.0 * (jnp.concatenate([own_ids, other_ids]) + 1).astype(F32) / HEADS)

    mine_out = lax.dynamic_slice_in_dim(w_out, zero_from(mine_cot), half, 0)
    out_first = gather_first(mine_out)
    tree_unit, _ = normalise(tree.astype(F32))
    normed = (tree_unit * gain_one + shift_one).astype(BF16)
    qkv = (dot_nn(normed, w_heads) + head_shift).astype(BF16)
    qkv, *out_first = gate([qkv, *out_first])
    out_second = gather_second(out_first)
    mixed = attend(order, slopes, qkv)
    mixed, mine_cot, *rest = gate(
        [mixed, mine_cot, *down_pieces, *out_first, *out_second, *up_blocks]
    )
    down_pieces, rest = rest[:groups], rest[groups:]
    out_first, rest = rest[: len(out_first)], rest[len(out_first) :]
    out_second, up_blocks = rest[: len(out_second)], rest[len(out_second) :]
    out_own = place(gather_blocks(mine_out, out_first, out_second), 1)
    up_own = place(up_blocks, 0)
    up_other, out_other = swap_cores(up_own), swap_cores(out_own)

    arrived = [rows_of(mixed, 0)]
    for k in range(1, planes):
        arrived.append(ring_send(rows_of(mixed, k), k))
    cot_first = gather_first(mine_cot)
    down_pieces = list(gate(down_pieces, arrived[1]))
    early = range(1, 3) if groups == 4 else range(1, groups)
    down_blocks = down_pieces[:1] + [xor_send(down_pieces[k], k) for k in early]
    out_other, *rest = gate([out_other, *arrived, *cot_first])
    arrived, cot_first = rest[:planes], rest[planes:]
    cot_second = gather_second(cot_first)
    attended = jnp.stack(arrived[::-1], axis=0)
    attended = jnp.roll(attended, plane + 1, axis=0)
    attended = attended.reshape(planes, rows, 2, columns).transpose(2, 1, 0, 3)
    attended = attended.reshape(2, rows, half)
    middle = mine.astype(F32) + (
        dot_nn(attended[0], out_own) + dot_nn(attended[1], out_other) + out_shift
    )
    unit_two, scale_two = normalise(middle)
    normed_two = (unit_two * gain_two + shift_two).astype(BF16)
    (normed_two,) = gate([normed_two], *cot_second, *down_blocks[1:])
    two_first = gather_first(normed_two)
    rest = gate([*two_first, *down_pieces])
    two_first, down_pieces = rest[: len(two_first)], rest[len(two_first) :]
    two_second = gather_second(two_first)
    down_blocks += [xor_send(down_pieces[k], k) for k in range(len(down_blocks), groups)]
    all_two = jnp.concatenate(gather_blocks(normed_two, two_first, two_second), axis=0)
    all_cot = jnp.concatenate(gather_blocks(mine_cot, cot_first, cot_second), axis=0)

    pre_other = dot_nn(all_two, up_other) + up_shift[1:2]
    active_other = (pre_other * normal_cdf(pre_other)).astype(BF16)
    grad_down = swap_cores(dot_tn(active_other, all_cot).astype(BF16))
    pre_own = dot_nn(all_two, up_own) + up_shift[0:1]
    active_own = (pre_own * normal_cdf(pre_own)).astype(BF16)
    grad_down = (dot_tn(active_own, all_cot) + grad_down.astype(F32)).astype(BF16)

    def slope_of(pre):
        return normal_cdf(pre) + pre * normal_pdf(pre)

    (down_blocks[-1],) = gate(down_blocks[-1:], grad_down)
    down_own = place(down_blocks, 1)
    down_other = swap_cores(down_own)
    back_own = (dot_nt(all_cot, down_own) * slope_of(pre_own)).astype(BF16)
    back_other = (dot_nt(all_cot, down_other) * slope_of(pre_other)).astype(BF16)

    grad_two = (dot_nt(back_own, up_own) + dot_nt(back_other, up_other)).astype(BF16)
    back_other_in = back_other
    back_other, own_two, *sent = gate(
        [back_other] + [grad_two[k * rows : (k + 1) * rows] for k in range(groups)]
    )
    grad_down = lax.psum_scatter(grad_down, "context", scatter_dimension=0, tiled=True)
    grad_two = send_blocks(sent)
    grad_up = swap_cores(dot_tn(all_two, back_other).astype(BF16))
    (grad_up,) = gate([grad_up], grad_two[0])
    grad_up = (dot_tn(all_two, back_own) + grad_up.astype(F32)).astype(BF16)
    grad_up = grad_up.reshape(groups, planes, part // planes, hidden).transpose(1, 0, 2, 3)
    grad_up = grad_up.reshape(width, hidden)
    grad_down, *grad_two = gate([grad_down, *grad_two], grad_up)
    grad_up = lax.psum_scatter(grad_up, "context", scatter_dimension=0, tiled=True)

    grad_two = add_up(own_two, grad_two)
    grad_middle = mine_cot.astype(F32) + norm_back(unit_two, scale_two, gain_two, grad_two)
    grad_branch = grad_middle.astype(BF16)
    grad_mixed = jnp.stack(
        [
            dot_nt(grad_branch, out_own).astype(BF16).reshape(rows, planes, columns),
            dot_nt(grad_branch, out_other).astype(BF16).reshape(rows, planes, columns),
        ],
        axis=1,
    )
    grad_mixed = grad_mixed.transpose(2, 0, 1, 3).reshape(planes, rows, 2 * columns)
    grad_mixed = jnp.roll(grad_mixed, -plane, axis=0)
    grad_out = swap_cores(dot_tn(attended[1], grad_branch).astype(BF16))
    grad_out = dot_tn(attended[0], grad_branch) + grad_out.astype(F32)
    out_own_block, *rest = gate(
        [pick(grad_out, 0, 1)]
        + [pick(grad_out, k, 1).astype(BF16) for k in range(1, groups)]
        + [grad_mixed[k] for k in range(planes)]
    )
    out_blocks, grad_mixed = rest[: groups - 1], rest[groups - 1 :]

    back_rows = [grad_mixed[0]]
    for k in range(1, planes):
        back_rows.append(ring_send(grad_mixed[k], k))
    grad_out = add_up(out_own_block, send_blocks(out_blocks)).astype(BF16)
    grad_tree = jnp.roll(jnp.stack(back_rows[:1] + back_rows[:0:-1]), plane, axis=0)
    grad_tree = grad_tree.reshape(planes * rows, 2 * columns)
    grad_tree, grad_up, grad_down, grad_out = gate([grad_tree, grad_up, grad_down, grad_out])
    grad_out = lax.psum_scatter(grad_out, "context", scatter_dimension=0, tiled=True)

    lines = grad_down.shape[0]
    grad_up = grad_up.reshape(groups, lines // (hidden // part), hidden)
    both = []
    for k in range(groups):
        piece = pick(grad_up, k, 0)[0]
        piece = [piece[:, i : i + part] for i in range(0, hidden, part)]
        both.append(jnp.concatenate([pick(grad_down, k, 1), *piece]))
    both = both[:1] + send_blocks(both[1:])
    grad_qkv = attend_back(order, slopes, qkv, grad_tree)
    grad_qkv, grad_out, *both = gate([grad_qkv, grad_out, *both])
    g_out = lax.all_gather(grad_out, "context", axis=0, tiled=True)
    grad_down = place([piece[None, :lines] for piece in both], 0)
    g_up = jnp.concatenate([piece[lines:] for piece in both])
    g_up = lax.all_gather(g_up, "context", axis=0, tiled=True)
    down_up, down_down = line_step([grad_down], [grad_down])

    grad_normed = dot_nt(grad_qkv, w_heads)
    head_sums = jnp.sum(grad_qkv.astype(F32), axis=0).reshape(2, pairs, 3, PAIR)
    head_sums = jnp.stack([head_sums[:, :, 0], head_sums[:, :, 2]], axis=1)
    head_row = lax.dynamic_update_slice_in_dim(
        jnp.zeros((2, 2, half), F32), head_sums.reshape(2, 2, columns), plane * columns, 2
    )
    up_sums = [jnp.sum(side.astype(F32), axis=0) for side in (back_own, back_other_in)]
    sums = jnp.concatenate(
        [
            jnp.sum(grad_normed * tree_unit, axis=0),
            jnp.sum(grad_two * unit_two, axis=0),
            jnp.sum(grad_normed, axis=0),
            jnp.sum(grad_two, axis=0),
            jnp.sum(grad_branch.astype(F32), axis=0),
            jnp.sum(mine_cot.astype(F32), axis=0),
            head_row.reshape(-1),
            *up_sums,
        ]
    )
    lines = -(-sums.shape[0] // (16 * width)) * 16
    sums = jnp.pad(sums, (0, lines * width - sums.shape[0])).reshape(lines, width)
    blocks = [
        jnp.concatenate([grad_normed[k * rows : (k + 1) * rows], sums]) for k in range(planes)
    ]
    blocks = jnp.concatenate(blocks).astype(BF16)
    blocks, grad_qkv, down_up[-1], down_down[-1] = gate(
        [blocks, grad_qkv, down_up[-1], down_down[-1]], g_out
    )
    later = zero_from(blocks)
    grad_first = lax.psum_scatter(blocks, "context", scatter_dimension=0, tiled=True)

    down_up, down_down = line_step(down_up, down_down)
    grad_heads = dot_tn(normed, grad_qkv)
    head_other = swap_cores(grad_heads[:, 3 * columns :].astype(BF16))
    grad_heads = grad_heads[:, : 3 * columns] + head_other.astype(F32)
    head_pieces = [pick(grad_heads, k, 0).astype(BF16) for k in range(1, groups)]
    grad_heads = add_up(pick(grad_heads, 0, 0), send_blocks(head_pieces)).astype(BF16)
    grad_heads = grad_heads.reshape(part, pairs, 3, PAIR).transpose(2, 0, 1, 3)
    grad_heads = grad_heads.reshape(3 * part, columns)
    layer_out = dot_nn(
        lax.dynamic_slice_in_dim(active_own, later, groups * rows, 0), down_own
    ) + dot_nn(lax.dynamic_slice_in_dim(active_other, later, groups * rows, 0), down_other)
    layer_out = layer_out.astype(BF16)
    grad_heads, down_up[-1], down_down[-1], *layer_blocks = gate(
        [grad_heads, down_up[-1], down_down[-1]]
        + [layer_out[k * rows : (k + 1) * rows] for k in range(groups)]
    )
    while len(down_up) < planes:
        down_up, down_down = line_step(down_up, down_down)
    layer_blocks[1:] = send_blocks(layer_blocks[1:])
    grad_first, grad_heads, g_up, g_out = gate(
        [grad_first, grad_heads, g_up, g_out],
        down_up[-1],
        down_down[-1],
        *layer_blocks[1:],
    )
    layer_out = middle + (add_up(layer_blocks[0], layer_blocks[1:]) + down_shift)
    layer_out = both_micros(layer_out.astype(BF16))

    g_heads = lax.all_gather(grad_heads, "context", axis=1, tiled=True)
    ordered = jnp.zeros((part, groups * hidden), F32)
    g_up = g_up.reshape(planes, groups, hidden // part, -1, part)
    for k in range(groups):
        for i in range(hidden // part):
            ordered = lax.dynamic_update_slice_in_dim(
                ordered,
                g_up[:, k, i].reshape(part, part).astype(F32),
                (group ^ k) * hidden + i * part,
                1,
            )
    g_up = ordered
    g_down = jnp.zeros((groups, planes, hidden // planes, part), F32)
    for k, piece in enumerate(line_blocks(down_up, down_down)):
        g_down = lax.dynamic_update_slice_in_dim(
            g_down, piece.astype(F32)[:, None], (plane + k) % planes, 1
        )

    sums = grad_first[rows:].astype(F32).reshape(-1)
    grad_first = grad_first[:rows].astype(F32)
    unit_one, scale_one = normalise(mine.astype(F32))
    grad_tokens = grad_middle + norm_back(unit_one, scale_one, gain_one, grad_first)
    grad_tokens = both_micros(grad_tokens.astype(BF16))

    spread = sums[: 6 * width].reshape(6, groups, part)
    spread = spread.transpose(1, 0, 2).reshape(groups, 6 * part)
    head_row = sums[6 * width : 8 * width].reshape(4, groups, part // 2)
    head_row = head_row.transpose(1, 0, 2).reshape(groups, 2 * part)
    up_sums = sums[8 * width : 8 * width + 2 * hidden].reshape(2, hidden)
    sums = jnp.concatenate([spread, head_row], axis=1)
    total = pick(sums, 0, 0)
    for k in range(1, groups):
        total = total + xor_send(pick(sums, k, 0), k)
    total = total[0]
    total_other = swap_cores(jnp.concatenate([total[: 6 * part], total[7 * part :], up_sums[1]]))
    total = jnp.concatenate([total[: 7 * part], up_sums[0]]) + total_other
    wide = total[: 6 * part].reshape(6, part)
    return (
        layer_out,
        grad_tokens,
        wide[0:2],
        wide[2:4],
        g_heads.astype(F32).reshape(3, part, half),
        total[6 * part : 7 * part].reshape(2, part // 2),
        g_out.astype(F32),
        wide[4],
        g_up,
        total[7 * part :],
        g_down.reshape(groups * hidden, part),
        wide[5],
    )


def solution(mesh):
    rows = P(None, ("fsdp", "context"), None)
    params = (
        P(None, "fsdp"),
        P(None, "fsdp"),
        P(None, "fsdp", "tensor"),
        P(None, ("tensor", "fsdp")),
        P("tensor", "fsdp"),
        P("fsdp"),
        P("fsdp", "tensor"),
        P(("tensor", "fsdp")),
        P("tensor", "fsdp"),
        P("fsdp"),
    )
    in_specs = (rows, rows, P(None, "fsdp"), P(None, "fsdp")) + params
    return jax.shard_map(
        per_device, mesh=mesh, in_specs=in_specs, out_specs=(rows, rows) + params, check_vma=False
    )
```

```python
from functools import partial

import jax
import jax.numpy as jnp
from jax import lax
from jax.experimental import pallas as pl
from jax.experimental.pallas import tpu as pltpu
from jax.sharding import PartitionSpec as P

HEADS = 32
HEAD_DIM = 64
SEG = 128
TREE_SEGS = 8
LAST_DEPTH = 6
MICRO = 2
PAIR = 2 * HEAD_DIM
NEG_FILL = -1e30
F32 = jnp.float32
BF16 = jnp.bfloat16


def dot_nn(left, right):
    return lax.dot_general(left, right, (((1,), (0,)), ((), ())), preferred_element_type=F32)


def dot_tn(left, right):
    return lax.dot_general(left, right, (((0,), (0,)), ((), ())), preferred_element_type=F32)


def dot_nt(left, right):
    return lax.dot_general(left, right, (((1,), (1,)), ((), ())), preferred_element_type=F32)


def swap_cores(value):
    return lax.ppermute(value, "tensor", [(0, 1), (1, 0)])


def xor_send(value, step):
    size = lax.axis_size("fsdp")
    return lax.ppermute(value, "fsdp", [(i, i ^ step) for i in range(size)])


def ring_send(value, step):
    size = lax.axis_size("context")
    return lax.ppermute(value, "context", [(i, (i + step) % size) for i in range(size)])


def line_step(upward, downward):
    size, step = lax.axis_size("context"), len(upward)
    above = lax.ppermute(upward[-1], "context", [(i, i + 1) for i in range(step - 1, size - 1)])
    below = lax.ppermute(downward[-1], "context", [(i + 1, i) for i in range(0, size - step)])
    return upward + [above], downward + [below]


def line_blocks(upward, downward):
    size, index = lax.axis_size("context"), lax.axis_index("context")
    blocks = [upward[0]]
    for k in range(1, size):
        blocks.append(jnp.where(index + k < size, downward[k], upward[size - k]))
    return blocks


def pass_on(*refs):
    pass


def corner(value):
    limits = [1] * (value.ndim - 2) + [8, 128]
    return lax.slice(value, [0] * value.ndim, limits).reshape(8, 128).astype(F32)


def gate(values, *earlier):
    if earlier:
        earlier = (sum([corner(value) for value in earlier[1:]], corner(earlier[0])),)
    anywhere = pl.BlockSpec(memory_space=pl.ANY)
    return pl.pallas_call(
        pass_on,
        out_shape=[jax.ShapeDtypeStruct(value.shape, value.dtype) for value in values],
        in_specs=[anywhere] * (len(values) + len(earlier)),
        out_specs=[anywhere] * len(values),
        input_output_aliases={i: i for i in range(len(values))},
        compiler_params=pltpu.CompilerParams(vmem_limit_bytes=1 << 20),
        cost_estimate=pl.CostEstimate(flops=1, transcendentals=0, bytes_accessed=1),
        name="gate",
    )(*values, *earlier)


def zero_from(value):
    first = value[(slice(0, 1),) * value.ndim].reshape(())
    return jnp.minimum(jnp.abs(first.astype(F32)).astype(jnp.int32), 0)


def gather_first(value):
    size = lax.axis_size("fsdp")
    return [xor_send(value, k) for k in ((1, 2) if size == 4 else range(1, size))]


def gather_second(blocks):
    if lax.axis_size("fsdp") != 4:
        return []
    middle = blocks[0].shape[0] // 2
    return [xor_send(blocks[1][:middle], 1), xor_send(blocks[0][middle:], 2)]


def gather_blocks(value, first, second):
    return [value, *first] + ([jnp.concatenate(second, axis=0)] if second else [])


def place(pieces, axis, offset=0):
    index = lax.axis_index("fsdp")
    width = pieces[0].shape[axis]
    shape = list(pieces[0].shape)
    shape[axis] = width * len(pieces)
    whole = jnp.zeros(shape, pieces[0].dtype)
    for k, piece in enumerate(pieces):
        whole = lax.dynamic_update_slice_in_dim(whole, piece, (index ^ k) * width + offset, axis)
    return whole


def pick(whole, k, axis, offset=0):
    width = whole.shape[axis] // lax.axis_size("fsdp")
    start = (lax.axis_index("fsdp") ^ k) * width + offset
    return lax.dynamic_slice_in_dim(whole, start, width, axis)


def exchange(whole, axis, offset=0):
    blocks = [pick(whole, 0, axis, offset)]
    for k in range(1, lax.axis_size("fsdp")):
        blocks.append(xor_send(pick(whole, k, axis, offset), k))
    return blocks


def send_blocks(pieces):
    return [xor_send(piece, k) for k, piece in enumerate(pieces, 1)]


def add_up(own, pieces):
    return sum([piece.astype(F32) for piece in pieces], own.astype(F32))


def head_lanes(rows):
    return lax.broadcasted_iota(jnp.int32, (rows, PAIR), 1) < HEAD_DIM


def split_heads(value):
    first = head_lanes(value.shape[0])
    zero = jnp.zeros_like(value)
    return jnp.concatenate([jnp.where(first, value, zero), jnp.where(first, zero, value)], axis=0)


def join_heads(stacked):
    first = head_lanes(SEG)
    return jnp.where(first, stacked[:SEG], stacked[SEG:])


def probabilities(stacked_queries, keys, block, slope_a, slope_b):
    width = (block + 1) * SEG
    scores = dot_nt(stacked_queries, keys)
    row = lax.broadcasted_iota(jnp.int32, (2 * SEG, 1), 0)
    column = lax.broadcasted_iota(jnp.int32, (1, width), 1)
    local = jnp.where(row < SEG, row, row - SEG)
    slope = jnp.where(row < SEG, slope_a, slope_b)
    place_row = local + min(block, LAST_DEPTH) * SEG
    place_column = jnp.where(column < (LAST_DEPTH + 1) * SEG, column, column - SEG)
    scores = scores + slope * (place_column - place_row).astype(F32)
    allowed = column <= local + block * SEG
    if block == LAST_DEPTH + 1:
        allowed = allowed & ((column < LAST_DEPTH * SEG) | (column >= (LAST_DEPTH + 1) * SEG))
    scores = jnp.where(allowed, scores, NEG_FILL)
    raised = jnp.exp(scores - jnp.max(scores, axis=-1, keepdims=True))
    return raised * (1.0 / jnp.sum(raised, axis=-1, keepdims=True))


def attention_forward(order, slopes, qkv_ref, out_ref, keys, values):
    pair = pl.program_id(0)
    slope_a, slope_b = slopes[2 * pair], slopes[2 * pair + 1]
    for block in range(TREE_SEGS):
        rows = pl.ds(block * SEG, SEG)
        keys[rows, :] = qkv_ref[order[block], :, PAIR : 2 * PAIR]
        values[rows, :] = qkv_ref[order[block], :, 2 * PAIR : 3 * PAIR]
    for block in range(TREE_SEGS):
        seen = pl.ds(0, (block + 1) * SEG)
        queries = split_heads(qkv_ref[order[block], :, :PAIR] * BF16(HEAD_DIM**-0.5))
        probs = probabilities(queries, keys[seen, :], block, slope_a, slope_b)
        mixed = dot_nn(probs.astype(BF16), values[seen, :])
        out_ref[order[block]] = join_heads(mixed).astype(BF16)


def attention_backward(order, slopes, qkv_ref, grad_ref, out_ref, keys, values, grad_keys, grad_values):
    pair = pl.program_id(0)
    slope_a, slope_b = slopes[2 * pair], slopes[2 * pair + 1]
    for block in range(TREE_SEGS):
        rows = pl.ds(block * SEG, SEG)
        keys[rows, :] = qkv_ref[order[block], :, PAIR : 2 * PAIR]
        values[rows, :] = qkv_ref[order[block], :, 2 * PAIR : 3 * PAIR]
    grad_keys[...] = jnp.zeros_like(grad_keys)
    grad_values[...] = jnp.zeros_like(grad_values)
    for block in range(TREE_SEGS):
        seen = pl.ds(0, (block + 1) * SEG)
        queries = split_heads(qkv_ref[order[block], :, :PAIR] * BF16(HEAD_DIM**-0.5))
        grads = split_heads(grad_ref[order[block]])
        probs = probabilities(queries, keys[seen, :], block, slope_a, slope_b)
        grad_probs = dot_nt(grads, values[seen, :])
        centre = jnp.sum(probs * grad_probs, axis=-1, keepdims=True)
        grad_scores = (probs * (grad_probs - centre)).astype(BF16)
        grad_queries = join_heads(dot_nn(grad_scores, keys[seen, :])) * HEAD_DIM**-0.5
        out_ref[order[block], :, :PAIR] = grad_queries.astype(BF16)
        grad_keys[seen, :] += dot_tn(grad_scores, queries)
        grad_values[seen, :] += dot_tn(probs.astype(BF16), grads)
    for block in range(TREE_SEGS):
        rows = pl.ds(block * SEG, SEG)
        out_ref[order[block], :, PAIR : 2 * PAIR] = grad_keys[rows, :].astype(BF16)
        out_ref[order[block], :, 2 * PAIR : 3 * PAIR] = grad_values[rows, :].astype(BF16)


def block_of(width):
    return pl.BlockSpec((TREE_SEGS, SEG, width), lambda pair, *scalars: (0, 0, pair))


def attend(order, slopes, qkv):
    pairs = qkv.shape[1] // (3 * PAIR)
    rows = TREE_SEGS * SEG
    out = pl.pallas_call(
        attention_forward,
        out_shape=jax.ShapeDtypeStruct((TREE_SEGS, SEG, pairs * PAIR), BF16),
        grid_spec=pltpu.PrefetchScalarGridSpec(
            num_scalar_prefetch=2,
            grid=(pairs,),
            in_specs=[block_of(3 * PAIR)],
            out_specs=block_of(PAIR),
            scratch_shapes=[pltpu.VMEM((rows, PAIR), BF16)] * 2,
        ),
        compiler_params=pltpu.CompilerParams(vmem_limit_bytes=48 << 20),
        cost_estimate=pl.CostEstimate(
            flops=pairs * 32 * rows * rows * PAIR, transcendentals=0, bytes_accessed=1
        ),
        name="attend",
    )(order, slopes, qkv.reshape(TREE_SEGS, SEG, -1))
    return out.reshape(rows, pairs * PAIR)


def attend_back(order, slopes, qkv, grad):
    pairs = qkv.shape[1] // (3 * PAIR)
    rows = TREE_SEGS * SEG
    out = pl.pallas_call(
        attention_backward,
        out_shape=jax.ShapeDtypeStruct((TREE_SEGS, SEG, pairs * 3 * PAIR), BF16),
        grid_spec=pltpu.PrefetchScalarGridSpec(
            num_scalar_prefetch=2,
            grid=(pairs,),
            in_specs=[block_of(3 * PAIR), block_of(PAIR)],
            out_specs=block_of(3 * PAIR),
            scratch_shapes=[pltpu.VMEM((rows, PAIR), BF16)] * 2 + [pltpu.VMEM((rows, PAIR), F32)] * 2,
        ),
        compiler_params=pltpu.CompilerParams(vmem_limit_bytes=48 << 20),
        cost_estimate=pl.CostEstimate(
            flops=pairs * 60 * rows * rows * PAIR, transcendentals=0, bytes_accessed=1
        ),
        name="attend_back",
    )(order, slopes, qkv.reshape(TREE_SEGS, SEG, -1), grad.reshape(TREE_SEGS, SEG, -1))
    return out.reshape(rows, pairs * 3 * PAIR)


def normalise(rows):
    centred = rows - jnp.mean(rows, axis=-1, keepdims=True)
    scale = lax.rsqrt(jnp.mean(centred * centred, axis=-1, keepdims=True) + 1e-05)
    return centred * scale, scale


def norm_back(unit, scale, gain, upstream):
    weighted = upstream * gain
    centre = jnp.mean(weighted, axis=-1, keepdims=True)
    along = jnp.mean(weighted * unit, axis=-1, keepdims=True)
    return scale * (weighted - centre - unit * along)


def normal_cdf(value):
    return 0.5 * (1.0 + lax.erf(value * 0.7071067811865476))


def normal_pdf(value):
    return 0.3989422804014327 * jnp.exp(-0.5 * value * value)


def both_micros(mine):
    other = swap_cores(mine)
    first = lax.axis_index("tensor") == 0
    return jnp.stack([jnp.where(first, mine, other), jnp.where(first, other, mine)])


def per_device(
    tokens,
    cotangent,
    seg_parent,
    positions,
    norm_gain,
    norm_bias,
    w_qkv,
    bias_qv,
    w_out,
    bias_out,
    w_up,
    bias_up,
    w_down,
    bias_down,
):
    planes, groups = lax.axis_size("context"), lax.axis_size("fsdp")
    plane, group, core = (lax.axis_index(name) for name in ("context", "fsdp", "tensor"))
    rows, width = tokens.shape[1], tokens.shape[2]
    part = width // groups
    half = w_qkv.shape[2]
    columns = half // planes
    pairs = columns // PAIR
    hidden = w_up.shape[1] // groups

    def rows_of(whole, k):
        return lax.dynamic_slice_in_dim(whole, ((plane + k) % planes) * rows, rows, 0)

    mine = lax.dynamic_index_in_dim(tokens, core, 0, keepdims=False)
    mine_cot = lax.dynamic_index_in_dim(cotangent, core, 0, keepdims=False)
    packed = jnp.concatenate(
        [
            norm_gain,
            norm_bias,
            bias_out[None],
            bias_down[None],
            bias_qv.reshape(1, part),
            bias_up.reshape(-1, part),
        ],
        axis=0,
    )
    lines = packed.size // (3 * columns)
    chosen = lax.dynamic_slice_in_dim(w_qkv, plane * columns, columns, 2)
    chosen = chosen.reshape(3, part, pairs, PAIR).transpose(1, 2, 0, 3).reshape(part, 3 * columns)
    chosen = jnp.concatenate(
        [
            chosen,
            packed.reshape(lines, 3 * columns),
            jnp.zeros((-lines % 32, 3 * columns), BF16),
        ],
        axis=0,
    )
    up_pieces = [pick(w_up, k, 1) for k in range(groups)]
    down_pieces = [pick(w_down, k, 0) for k in range(groups)]

    tree = lax.all_gather(mine, "context", axis=0, tiled=True)
    head_first = gather_first(chosen)
    rest = gate([*head_first, *up_pieces[1:]])
    head_first, up_pieces[1:] = rest[: len(head_first)], rest[len(head_first) :]
    head_second = gather_second(head_first)
    up_blocks = up_pieces[:1] + send_blocks(up_pieces[1:])
    tree, mine_cot, *down_pieces = gate([tree, mine_cot, *down_pieces], *head_second)
    head_blocks = gather_blocks(chosen, head_first, head_second)
    heads_own = place([block[:part] for block in head_blocks], 0)
    w_heads = jnp.concatenate([heads_own, swap_cores(heads_own)], axis=1)

    small = [block[part : part + lines].reshape(1, -1, part) for block in head_blocks]
    small = place(small, 0)
    small = jnp.stack([small, swap_cores(small)])
    spread = small[0, :, :6].astype(F32).transpose(1, 0, 2).reshape(6, width)
    gain_one, gain_two, shift_one, shift_two, out_shift, down_shift = (
        spread[i : i + 1] for i in range(6)
    )
    head_shift = small[:, :, 6].astype(F32).reshape(2, groups, 2, part // 2).transpose(0, 2, 1, 3)
    head_shift = lax.dynamic_slice_in_dim(
        head_shift.reshape(2, 2, half), plane * columns, columns, 2
    ).reshape(2, 2, pairs, PAIR)
    head_shift = jnp.stack(
        [head_shift[:, 0], jnp.zeros_like(head_shift[:, 0]), head_shift[:, 1]], axis=2
    ).reshape(1, 2 * pairs * 3 * PAIR)
    up_shift = lax.dynamic_index_in_dim(small, group, 1, keepdims=False)[:, 7:]
    up_shift = up_shift.astype(F32).reshape(2, hidden)

    depth = lax.dynamic_index_in_dim(positions, core, 0, keepdims=False)[::SEG] // SEG
    ids = jnp.arange(TREE_SEGS, dtype=jnp.int32)
    before = (depth[None, :] < depth[:, None]) | (
        (depth[None, :] == depth[:, None]) & (ids[None, :] < ids[:, None])
    )
    rank = jnp.sum(before.astype(jnp.int32), axis=1)
    order = jnp.sum(jnp.where(rank[None, :] == ids[:, None], ids[None, :], 0), axis=1)
    local_heads = columns // HEAD_DIM
    head_ids = plane * local_heads + jnp.arange(local_heads, dtype=jnp.int32)
    own_ids = core * (half // HEAD_DIM) + head_ids
    other_ids = (1 - core) * (half // HEAD_DIM) + head_ids
    slopes = jnp.exp2(-8.0 * (jnp.concatenate([own_ids, other_ids]) + 1).astype(F32) / HEADS)

    mine_out = lax.dynamic_slice_in_dim(w_out, zero_from(mine_cot), half, 0)
    out_first = gather_first(mine_out)
    tree_unit, _ = normalise(tree.astype(F32))
    normed = (tree_unit * gain_one + shift_one).astype(BF16)
    qkv = (dot_nn(normed, w_heads) + head_shift).astype(BF16)
    qkv, *out_first = gate([qkv, *out_first])
    out_second = gather_second(out_first)
    mixed = attend(order, slopes, qkv)
    mixed, mine_cot, *rest = gate(
        [mixed, mine_cot, *down_pieces, *out_first, *out_second, *up_blocks]
    )
    down_pieces, rest = rest[:groups], rest[groups:]
    out_first, rest = rest[: len(out_first)], rest[len(out_first) :]
    out_second, up_blocks = rest[: len(out_second)], rest[len(out_second) :]
    out_own = place(gather_blocks(mine_out, out_first, out_second), 1)
    up_own = place(up_blocks, 0)
    up_other, out_other = swap_cores(up_own), swap_cores(out_own)

    arrived = [rows_of(mixed, 0)]
    for k in range(1, planes):
        arrived.append(ring_send(rows_of(mixed, k), k))
    cot_first = gather_first(mine_cot)
    down_pieces = list(gate(down_pieces, arrived[1]))
    early = range(1, 3) if groups == 4 else range(1, groups)
    down_blocks = down_pieces[:1] + [xor_send(down_pieces[k], k) for k in early]
    out_other, *rest = gate([out_other, *arrived, *cot_first])
    arrived, cot_first = rest[:planes], rest[planes:]
    cot_second = gather_second(cot_first)
    attended = jnp.stack(arrived[::-1], axis=0)
    attended = jnp.roll(attended, plane + 1, axis=0)
    attended = attended.reshape(planes, rows, 2, columns).transpose(2, 1, 0, 3)
    attended = attended.reshape(2, rows, half)
    middle = mine.astype(F32) + (
        dot_nn(attended[0], out_own) + dot_nn(attended[1], out_other) + out_shift
    )
    unit_two, scale_two = normalise(middle)
    normed_two = (unit_two * gain_two + shift_two).astype(BF16)
    (normed_two,) = gate([normed_two], *cot_second, *down_blocks[1:])
    two_first = gather_first(normed_two)
    rest = gate([*two_first, *down_pieces])
    two_first, down_pieces = rest[: len(two_first)], rest[len(two_first) :]
    two_second = gather_second(two_first)
    down_blocks += [xor_send(down_pieces[k], k) for k in range(len(down_blocks), groups)]
    all_two = jnp.concatenate(gather_blocks(normed_two, two_first, two_second), axis=0)
    all_cot = jnp.concatenate(gather_blocks(mine_cot, cot_first, cot_second), axis=0)

    pre_other = dot_nn(all_two, up_other) + up_shift[1:2]
    active_other = (pre_other * normal_cdf(pre_other)).astype(BF16)
    grad_down = swap_cores(dot_tn(active_other, all_cot).astype(BF16))
    pre_own = dot_nn(all_two, up_own) + up_shift[0:1]
    active_own = (pre_own * normal_cdf(pre_own)).astype(BF16)
    grad_down = (dot_tn(active_own, all_cot) + grad_down.astype(F32)).astype(BF16)

    def slope_of(pre):
        return normal_cdf(pre) + pre * normal_pdf(pre)

    (down_blocks[-1],) = gate(down_blocks[-1:], grad_down)
    down_own = place(down_blocks, 1)
    down_other = swap_cores(down_own)
    back_own = (dot_nt(all_cot, down_own) * slope_of(pre_own)).astype(BF16)
    back_other = (dot_nt(all_cot, down_other) * slope_of(pre_other)).astype(BF16)

    grad_two = (dot_nt(back_own, up_own) + dot_nt(back_other, up_other)).astype(BF16)
    back_other_in = back_other
    back_other, own_two, *sent = gate(
        [back_other] + [grad_two[k * rows : (k + 1) * rows] for k in range(groups)]
    )
    grad_down = lax.psum_scatter(grad_down, "context", scatter_dimension=0, tiled=True)
    grad_two = send_blocks(sent)
    grad_up = swap_cores(dot_tn(all_two, back_other).astype(BF16))
    (grad_up,) = gate([grad_up], grad_two[0])
    grad_up = (dot_tn(all_two, back_own) + grad_up.astype(F32)).astype(BF16)
    grad_up = grad_up.reshape(groups, planes, part // planes, hidden).transpose(1, 0, 2, 3)
    grad_up = grad_up.reshape(width, hidden)
    grad_down, *grad_two = gate([grad_down, *grad_two], grad_up)
    grad_up = lax.psum_scatter(grad_up, "context", scatter_dimension=0, tiled=True)

    grad_two = add_up(own_two, grad_two)
    grad_middle = mine_cot.astype(F32) + norm_back(unit_two, scale_two, gain_two, grad_two)
    grad_branch = grad_middle.astype(BF16)
    grad_mixed = jnp.stack(
        [
            dot_nt(grad_branch, out_own).astype(BF16).reshape(rows, planes, columns),
            dot_nt(grad_branch, out_other).astype(BF16).reshape(rows, planes, columns),
        ],
        axis=1,
    )
    grad_mixed = grad_mixed.transpose(2, 0, 1, 3).reshape(planes, rows, 2 * columns)
    grad_mixed = jnp.roll(grad_mixed, -plane, axis=0)
    grad_out = swap_cores(dot_tn(attended[1], grad_branch).astype(BF16))
    grad_out = dot_tn(attended[0], grad_branch) + grad_out.astype(F32)
    out_own_block, *rest = gate(
        [pick(grad_out, 0, 1)]
        + [pick(grad_out, k, 1).astype(BF16) for k in range(1, groups)]
        + [grad_mixed[k] for k in range(planes)]
    )
    out_blocks, grad_mixed = rest[: groups - 1], rest[groups - 1 :]

    back_rows = [grad_mixed[0]]
    for k in range(1, planes):
        back_rows.append(ring_send(grad_mixed[k], k))
    grad_out = add_up(out_own_block, send_blocks(out_blocks)).astype(BF16)
    grad_tree = jnp.roll(jnp.stack(back_rows[:1] + back_rows[:0:-1]), plane, axis=0)
    grad_tree = grad_tree.reshape(planes * rows, 2 * columns)
    grad_tree, grad_up, grad_down, grad_out = gate([grad_tree, grad_up, grad_down, grad_out])
    grad_out = lax.psum_scatter(grad_out, "context", scatter_dimension=0, tiled=True)

    lines = grad_down.shape[0]
    grad_up = grad_up.reshape(groups, lines // (hidden // part), hidden)
    both = []
    for k in range(groups):
        piece = pick(grad_up, k, 0)[0]
        piece = [piece[:, i : i + part] for i in range(0, hidden, part)]
        both.append(jnp.concatenate([pick(grad_down, k, 1), *piece]))
    both = both[:1] + send_blocks(both[1:])
    grad_qkv = attend_back(order, slopes, qkv, grad_tree)
    grad_qkv, grad_out = gate([grad_qkv, grad_out], *both[1:])
    g_out = lax.all_gather(grad_out, "context", axis=0, tiled=True)
    g_up = jnp.concatenate([piece[lines:] for piece in both])
    grad_down = place([piece[None, :lines] for piece in both], 0, zero_from(g_up))
    g_up = lax.all_gather(g_up, "context", axis=0, tiled=True)
    down_up, down_down = line_step([grad_down], [grad_down])

    grad_normed = dot_nt(grad_qkv, w_heads)
    head_sums = jnp.sum(grad_qkv.astype(F32), axis=0).reshape(2, pairs, 3, PAIR)
    head_sums = jnp.stack([head_sums[:, :, 0], head_sums[:, :, 2]], axis=1)
    head_row = lax.dynamic_update_slice_in_dim(
        jnp.zeros((2, 2, half), F32), head_sums.reshape(2, 2, columns), plane * columns, 2
    )
    up_sums = [jnp.sum(side.astype(F32), axis=0) for side in (back_own, back_other_in)]
    sums = jnp.concatenate(
        [
            jnp.sum(grad_normed * tree_unit, axis=0),
            jnp.sum(grad_two * unit_two, axis=0),
            jnp.sum(grad_normed, axis=0),
            jnp.sum(grad_two, axis=0),
            jnp.sum(grad_branch.astype(F32), axis=0),
            jnp.sum(mine_cot.astype(F32), axis=0),
            head_row.reshape(-1),
            *up_sums,
        ]
    )
    lines = -(-sums.shape[0] // (16 * width)) * 16
    sums = jnp.pad(sums, (0, lines * width - sums.shape[0])).reshape(lines, width)
    blocks = [
        jnp.concatenate([grad_normed[k * rows : (k + 1) * rows], sums]) for k in range(planes)
    ]
    blocks = jnp.concatenate(blocks).astype(BF16)
    blocks, grad_qkv, down_up[-1], down_down[-1] = gate(
        [blocks, grad_qkv, down_up[-1], down_down[-1]], g_out
    )
    later = zero_from(blocks)
    grad_first = lax.psum_scatter(blocks, "context", scatter_dimension=0, tiled=True)

    down_up, down_down = line_step(down_up, down_down)
    grad_heads = dot_tn(normed, grad_qkv)
    head_other = swap_cores(grad_heads[:, 3 * columns :].astype(BF16))
    grad_heads = grad_heads[:, : 3 * columns] + head_other.astype(F32)
    head_pieces = [pick(grad_heads, k, 0).astype(BF16) for k in range(1, groups)]
    grad_heads = add_up(pick(grad_heads, 0, 0), send_blocks(head_pieces)).astype(BF16)
    grad_heads = grad_heads.reshape(part, pairs, 3, PAIR).transpose(2, 0, 1, 3)
    grad_heads = grad_heads.reshape(3 * part, columns)
    layer_out = dot_nn(
        lax.dynamic_slice_in_dim(active_own, later, groups * rows, 0), down_own
    ) + dot_nn(lax.dynamic_slice_in_dim(active_other, later, groups * rows, 0), down_other)
    layer_out = layer_out.astype(BF16)
    grad_heads, down_up[-1], down_down[-1], *layer_blocks = gate(
        [grad_heads, down_up[-1], down_down[-1]]
        + [layer_out[k * rows : (k + 1) * rows] for k in range(groups)]
    )
    while len(down_up) < planes:
        down_up, down_down = line_step(down_up, down_down)
    layer_blocks[1:] = send_blocks(layer_blocks[1:])
    grad_first, grad_heads, g_up, g_out = gate(
        [grad_first, grad_heads, g_up, g_out],
        down_up[-1],
        down_down[-1],
        *layer_blocks[1:],
    )
    layer_out = middle + (add_up(layer_blocks[0], layer_blocks[1:]) + down_shift)
    layer_out = both_micros(layer_out.astype(BF16))

    g_heads = lax.all_gather(grad_heads, "context", axis=1, tiled=True)
    ordered = jnp.zeros((part, groups * hidden), F32)
    g_up = g_up.reshape(planes, groups, hidden // part, -1, part)
    for k in range(groups):
        for i in range(hidden // part):
            ordered = lax.dynamic_update_slice_in_dim(
                ordered,
                g_up[:, k, i].reshape(part, part).astype(F32),
                (group ^ k) * hidden + i * part,
                1,
            )
    g_up = ordered
    g_down = jnp.zeros((groups, planes, hidden // planes, part), F32)
    for k, piece in enumerate(line_blocks(down_up, down_down)):
        g_down = lax.dynamic_update_slice_in_dim(
            g_down, piece.astype(F32)[:, None], (plane + k) % planes, 1
        )

    sums = grad_first[rows:].astype(F32).reshape(-1)
    grad_first = grad_first[:rows].astype(F32)
    unit_one, scale_one = normalise(mine.astype(F32))
    grad_tokens = grad_middle + norm_back(unit_one, scale_one, gain_one, grad_first)
    grad_tokens = both_micros(grad_tokens.astype(BF16))

    spread = sums[: 6 * width].reshape(6, groups, part)
    spread = spread.transpose(1, 0, 2).reshape(groups, 6 * part)
    head_row = sums[6 * width : 8 * width].reshape(4, groups, part // 2)
    head_row = head_row.transpose(1, 0, 2).reshape(groups, 2 * part)
    up_sums = sums[8 * width : 8 * width + 2 * hidden].reshape(2, hidden)
    sums = jnp.concatenate([spread, head_row], axis=1)
    total = pick(sums, 0, 0)
    for k in range(1, groups):
        total = total + xor_send(pick(sums, k, 0), k)
    total = total[0]
    total_other = swap_cores(jnp.concatenate([total[: 6 * part], total[7 * part :], up_sums[1]]))
    total = jnp.concatenate([total[: 7 * part], up_sums[0]]) + total_other
    wide = total[: 6 * part].reshape(6, part)
    return (
        layer_out,
        grad_tokens,
        wide[0:2],
        wide[2:4],
        g_heads.astype(F32).reshape(3, part, half),
        total[6 * part : 7 * part].reshape(2, part // 2),
        g_out.astype(F32),
        wide[4],
        g_up,
        total[7 * part :],
        g_down.reshape(groups * hidden, part),
        wide[5],
    )


def solution(mesh):
    rows = P(None, ("fsdp", "context"), None)
    params = (
        P(None, "fsdp"),
        P(None, "fsdp"),
        P(None, "fsdp", "tensor"),
        P(None, ("tensor", "fsdp")),
        P("tensor", "fsdp"),
        P("fsdp"),
        P("fsdp", "tensor"),
        P(("tensor", "fsdp")),
        P("tensor", "fsdp"),
        P("fsdp"),
    )
    in_specs = (rows, rows, P(None, "fsdp"), P(None, "fsdp")) + params
    return jax.shard_map(
        per_device, mesh=mesh, in_specs=in_specs, out_specs=(rows, rows) + params, check_vma=False
    )
```

```python
from functools import partial

import jax
import jax.numpy as jnp
from jax import lax
from jax.experimental import pallas as pl
from jax.experimental.pallas import tpu as pltpu
from jax.sharding import PartitionSpec as P

HEADS = 32
HEAD_DIM = 64
SEG = 128
TREE_SEGS = 8
LAST_DEPTH = 6
MICRO = 2
PAIR = 2 * HEAD_DIM
NEG_FILL = -1e30
F32 = jnp.float32
BF16 = jnp.bfloat16


def dot_nn(left, right):
    return lax.dot_general(left, right, (((1,), (0,)), ((), ())), preferred_element_type=F32)


def dot_tn(left, right):
    return lax.dot_general(left, right, (((0,), (0,)), ((), ())), preferred_element_type=F32)


def dot_nt(left, right):
    return lax.dot_general(left, right, (((1,), (1,)), ((), ())), preferred_element_type=F32)


def swap_cores(value):
    return lax.ppermute(value, "tensor", [(0, 1), (1, 0)])


def xor_send(value, step):
    size = lax.axis_size("fsdp")
    return lax.ppermute(value, "fsdp", [(i, i ^ step) for i in range(size)])


def ring_send(value, step):
    size = lax.axis_size("context")
    return lax.ppermute(value, "context", [(i, (i + step) % size) for i in range(size)])


def line_step(upward, downward):
    size, step = lax.axis_size("context"), len(upward)
    above = lax.ppermute(upward[-1], "context", [(i, i + 1) for i in range(step - 1, size - 1)])
    below = lax.ppermute(downward[-1], "context", [(i + 1, i) for i in range(0, size - step)])
    return upward + [above], downward + [below]


def line_blocks(upward, downward):
    size, index = lax.axis_size("context"), lax.axis_index("context")
    blocks = [upward[0]]
    for k in range(1, size):
        blocks.append(jnp.where(index + k < size, downward[k], upward[size - k]))
    return blocks


def pass_on(*refs):
    pass


def corner(value):
    limits = [1] * (value.ndim - 2) + [8, 128]
    return lax.slice(value, [0] * value.ndim, limits).reshape(8, 128).astype(F32)


def gate(values, *earlier):
    if earlier:
        earlier = (sum([corner(value) for value in earlier[1:]], corner(earlier[0])),)
    anywhere = pl.BlockSpec(memory_space=pl.ANY)
    return pl.pallas_call(
        pass_on,
        out_shape=[jax.ShapeDtypeStruct(value.shape, value.dtype) for value in values],
        in_specs=[anywhere] * (len(values) + len(earlier)),
        out_specs=[anywhere] * len(values),
        input_output_aliases={i: i for i in range(len(values))},
        compiler_params=pltpu.CompilerParams(vmem_limit_bytes=1 << 20),
        cost_estimate=pl.CostEstimate(flops=1, transcendentals=0, bytes_accessed=1),
        name="gate",
    )(*values, *earlier)


def zero_from(value):
    first = value[(slice(0, 1),) * value.ndim].reshape(())
    return jnp.minimum(jnp.abs(first.astype(F32)).astype(jnp.int32), 0)


def gather_first(value):
    size = lax.axis_size("fsdp")
    return [xor_send(value, k) for k in ((1, 2) if size == 4 else range(1, size))]


def gather_second(blocks):
    if lax.axis_size("fsdp") != 4:
        return []
    middle = blocks[0].shape[0] // 2
    return [xor_send(blocks[1][:middle], 1), xor_send(blocks[0][middle:], 2)]


def gather_blocks(value, first, second):
    return [value, *first] + ([jnp.concatenate(second, axis=0)] if second else [])


def place(pieces, axis, offset=0):
    index = lax.axis_index("fsdp")
    width = pieces[0].shape[axis]
    shape = list(pieces[0].shape)
    shape[axis] = width * len(pieces)
    whole = jnp.zeros(shape, pieces[0].dtype)
    for k, piece in enumerate(pieces):
        whole = lax.dynamic_update_slice_in_dim(whole, piece, (index ^ k) * width + offset, axis)
    return whole


def pick(whole, k, axis, offset=0):
    width = whole.shape[axis] // lax.axis_size("fsdp")
    start = (lax.axis_index("fsdp") ^ k) * width + offset
    return lax.dynamic_slice_in_dim(whole, start, width, axis)


def exchange(whole, axis, offset=0):
    blocks = [pick(whole, 0, axis, offset)]
    for k in range(1, lax.axis_size("fsdp")):
        blocks.append(xor_send(pick(whole, k, axis, offset), k))
    return blocks


def send_blocks(pieces):
    return [xor_send(piece, k) for k, piece in enumerate(pieces, 1)]


def add_up(own, pieces):
    return sum([piece.astype(F32) for piece in pieces], own.astype(F32))


def head_lanes(rows):
    return lax.broadcasted_iota(jnp.int32, (rows, PAIR), 1) < HEAD_DIM


def split_heads(value):
    first = head_lanes(value.shape[0])
    zero = jnp.zeros_like(value)
    return jnp.concatenate([jnp.where(first, value, zero), jnp.where(first, zero, value)], axis=0)


def join_heads(stacked):
    first = head_lanes(SEG)
    return jnp.where(first, stacked[:SEG], stacked[SEG:])


def probabilities(stacked_queries, keys, block, slope_a, slope_b):
    width = (block + 1) * SEG
    scores = dot_nt(stacked_queries, keys)
    row = lax.broadcasted_iota(jnp.int32, (2 * SEG, 1), 0)
    column = lax.broadcasted_iota(jnp.int32, (1, width), 1)
    local = jnp.where(row < SEG, row, row - SEG)
    slope = jnp.where(row < SEG, slope_a, slope_b)
    place_row = local + min(block, LAST_DEPTH) * SEG
    place_column = jnp.where(column < (LAST_DEPTH + 1) * SEG, column, column - SEG)
    scores = scores + slope * (place_column - place_row).astype(F32)
    allowed = column <= local + block * SEG
    if block == LAST_DEPTH + 1:
        allowed = allowed & ((column < LAST_DEPTH * SEG) | (column >= (LAST_DEPTH + 1) * SEG))
    scores = jnp.where(allowed, scores, NEG_FILL)
    raised = jnp.exp(scores - jnp.max(scores, axis=-1, keepdims=True))
    return raised * (1.0 / jnp.sum(raised, axis=-1, keepdims=True))


def attention_forward(order, slopes, qkv_ref, out_ref, keys, values):
    pair = pl.program_id(0)
    slope_a, slope_b = slopes[2 * pair], slopes[2 * pair + 1]
    for block in range(TREE_SEGS):
        rows = pl.ds(block * SEG, SEG)
        keys[rows, :] = qkv_ref[order[block], :, PAIR : 2 * PAIR]
        values[rows, :] = qkv_ref[order[block], :, 2 * PAIR : 3 * PAIR]
    for block in range(TREE_SEGS):
        seen = pl.ds(0, (block + 1) * SEG)
        queries = split_heads(qkv_ref[order[block], :, :PAIR] * BF16(HEAD_DIM**-0.5))
        probs = probabilities(queries, keys[seen, :], block, slope_a, slope_b)
        mixed = dot_nn(probs.astype(BF16), values[seen, :])
        out_ref[order[block]] = join_heads(mixed).astype(BF16)


def attention_backward(order, slopes, qkv_ref, grad_ref, out_ref, keys, values, grad_keys, grad_values):
    pair = pl.program_id(0)
    slope_a, slope_b = slopes[2 * pair], slopes[2 * pair + 1]
    for block in range(TREE_SEGS):
        rows = pl.ds(block * SEG, SEG)
        keys[rows, :] = qkv_ref[order[block], :, PAIR : 2 * PAIR]
        values[rows, :] = qkv_ref[order[block], :, 2 * PAIR : 3 * PAIR]
    grad_keys[...] = jnp.zeros_like(grad_keys)
    grad_values[...] = jnp.zeros_like(grad_values)
    for block in range(TREE_SEGS):
        seen = pl.ds(0, (block + 1) * SEG)
        queries = split_heads(qkv_ref[order[block], :, :PAIR] * BF16(HEAD_DIM**-0.5))
        grads = split_heads(grad_ref[order[block]])
        probs = probabilities(queries, keys[seen, :], block, slope_a, slope_b)
        grad_probs = dot_nt(grads, values[seen, :])
        centre = jnp.sum(probs * grad_probs, axis=-1, keepdims=True)
        grad_scores = (probs * (grad_probs - centre)).astype(BF16)
        grad_queries = join_heads(dot_nn(grad_scores, keys[seen, :])) * HEAD_DIM**-0.5
        out_ref[order[block], :, :PAIR] = grad_queries.astype(BF16)
        grad_keys[seen, :] += dot_tn(grad_scores, queries)
        grad_values[seen, :] += dot_tn(probs.astype(BF16), grads)
    for block in range(TREE_SEGS):
        rows = pl.ds(block * SEG, SEG)
        out_ref[order[block], :, PAIR : 2 * PAIR] = grad_keys[rows, :].astype(BF16)
        out_ref[order[block], :, 2 * PAIR : 3 * PAIR] = grad_values[rows, :].astype(BF16)


def block_of(width):
    return pl.BlockSpec((TREE_SEGS, SEG, width), lambda pair, *scalars: (0, 0, pair))


def attend(order, slopes, qkv):
    pairs = qkv.shape[1] // (3 * PAIR)
    rows = TREE_SEGS * SEG
    out = pl.pallas_call(
        attention_forward,
        out_shape=jax.ShapeDtypeStruct((TREE_SEGS, SEG, pairs * PAIR), BF16),
        grid_spec=pltpu.PrefetchScalarGridSpec(
            num_scalar_prefetch=2,
            grid=(pairs,),
            in_specs=[block_of(3 * PAIR)],
            out_specs=block_of(PAIR),
            scratch_shapes=[pltpu.VMEM((rows, PAIR), BF16)] * 2,
        ),
        compiler_params=pltpu.CompilerParams(vmem_limit_bytes=48 << 20),
        cost_estimate=pl.CostEstimate(
            flops=pairs * 32 * rows * rows * PAIR, transcendentals=0, bytes_accessed=1
        ),
        name="attend",
    )(order, slopes, qkv.reshape(TREE_SEGS, SEG, -1))
    return out.reshape(rows, pairs * PAIR)


def attend_back(order, slopes, qkv, grad):
    pairs = qkv.shape[1] // (3 * PAIR)
    rows = TREE_SEGS * SEG
    out = pl.pallas_call(
        attention_backward,
        out_shape=jax.ShapeDtypeStruct((TREE_SEGS, SEG, pairs * 3 * PAIR), BF16),
        grid_spec=pltpu.PrefetchScalarGridSpec(
            num_scalar_prefetch=2,
            grid=(pairs,),
            in_specs=[block_of(3 * PAIR), block_of(PAIR)],
            out_specs=block_of(3 * PAIR),
            scratch_shapes=[pltpu.VMEM((rows, PAIR), BF16)] * 2 + [pltpu.VMEM((rows, PAIR), F32)] * 2,
        ),
        compiler_params=pltpu.CompilerParams(vmem_limit_bytes=48 << 20),
        cost_estimate=pl.CostEstimate(
            flops=pairs * 60 * rows * rows * PAIR, transcendentals=0, bytes_accessed=1
        ),
        name="attend_back",
    )(order, slopes, qkv.reshape(TREE_SEGS, SEG, -1), grad.reshape(TREE_SEGS, SEG, -1))
    return out.reshape(rows, pairs * 3 * PAIR)


def normalise(rows):
    centred = rows - jnp.mean(rows, axis=-1, keepdims=True)
    scale = lax.rsqrt(jnp.mean(centred * centred, axis=-1, keepdims=True) + 1e-05)
    return centred * scale, scale


def norm_back(unit, scale, gain, upstream):
    weighted = upstream * gain
    centre = jnp.mean(weighted, axis=-1, keepdims=True)
    along = jnp.mean(weighted * unit, axis=-1, keepdims=True)
    return scale * (weighted - centre - unit * along)


def normal_cdf(value):
    return 0.5 * (1.0 + lax.erf(value * 0.7071067811865476))


def normal_pdf(value):
    return 0.3989422804014327 * jnp.exp(-0.5 * value * value)


def both_micros(mine):
    other = swap_cores(mine)
    first = lax.axis_index("tensor") == 0
    return jnp.stack([jnp.where(first, mine, other), jnp.where(first, other, mine)])


def per_device(
    tokens,
    cotangent,
    seg_parent,
    positions,
    norm_gain,
    norm_bias,
    w_qkv,
    bias_qv,
    w_out,
    bias_out,
    w_up,
    bias_up,
    w_down,
    bias_down,
):
    planes, groups = lax.axis_size("context"), lax.axis_size("fsdp")
    plane, group, core = (lax.axis_index(name) for name in ("context", "fsdp", "tensor"))
    rows, width = tokens.shape[1], tokens.shape[2]
    part = width // groups
    half = w_qkv.shape[2]
    columns = half // planes
    pairs = columns // PAIR
    hidden = w_up.shape[1] // groups

    def rows_of(whole, k):
        return lax.dynamic_slice_in_dim(whole, ((plane + k) % planes) * rows, rows, 0)

    mine = lax.dynamic_index_in_dim(tokens, core, 0, keepdims=False)
    mine_cot = lax.dynamic_index_in_dim(cotangent, core, 0, keepdims=False)
    packed = jnp.concatenate(
        [
            norm_gain,
            norm_bias,
            bias_out[None],
            bias_down[None],
            bias_qv.reshape(1, part),
            bias_up.reshape(-1, part),
        ],
        axis=0,
    )
    lines = packed.size // (3 * columns)
    chosen = lax.dynamic_slice_in_dim(w_qkv, plane * columns, columns, 2)
    chosen = chosen.reshape(3, part, pairs, PAIR).transpose(1, 2, 0, 3).reshape(part, 3 * columns)
    chosen = jnp.concatenate(
        [
            chosen,
            packed.reshape(lines, 3 * columns),
            jnp.zeros((-lines % 32, 3 * columns), BF16),
        ],
        axis=0,
    )
    up_pieces = [pick(w_up, k, 1) for k in range(groups)]
    down_pieces = [pick(w_down, k, 0) for k in range(groups)]

    tree = lax.all_gather(mine, "context", axis=0, tiled=True)
    head_first = gather_first(chosen)
    rest = gate([*head_first, *up_pieces[1:]])
    head_first, up_pieces[1:] = rest[: len(head_first)], rest[len(head_first) :]
    head_second = gather_second(head_first)
    up_blocks = up_pieces[:1] + send_blocks(up_pieces[1:])
    tree, mine_cot, *down_pieces = gate([tree, mine_cot, *down_pieces], *head_second)
    head_blocks = gather_blocks(chosen, head_first, head_second)
    heads_own = place([block[:part] for block in head_blocks], 0)
    w_heads = jnp.concatenate([heads_own, swap_cores(heads_own)], axis=1)

    small = [block[part : part + lines].reshape(1, -1, part) for block in head_blocks]
    small = place(small, 0)
    small = jnp.stack([small, swap_cores(small)])
    spread = small[0, :, :6].astype(F32).transpose(1, 0, 2).reshape(6, width)
    gain_one, gain_two, shift_one, shift_two, out_shift, down_shift = (
        spread[i : i + 1] for i in range(6)
    )
    head_shift = small[:, :, 6].astype(F32).reshape(2, groups, 2, part // 2).transpose(0, 2, 1, 3)
    head_shift = lax.dynamic_slice_in_dim(
        head_shift.reshape(2, 2, half), plane * columns, columns, 2
    ).reshape(2, 2, pairs, PAIR)
    head_shift = jnp.stack(
        [head_shift[:, 0], jnp.zeros_like(head_shift[:, 0]), head_shift[:, 1]], axis=2
    ).reshape(1, 2 * pairs * 3 * PAIR)
    up_shift = lax.dynamic_index_in_dim(small, group, 1, keepdims=False)[:, 7:]
    up_shift = up_shift.astype(F32).reshape(2, hidden)

    depth = lax.dynamic_index_in_dim(positions, core, 0, keepdims=False)[::SEG] // SEG
    ids = jnp.arange(TREE_SEGS, dtype=jnp.int32)
    before = (depth[None, :] < depth[:, None]) | (
        (depth[None, :] == depth[:, None]) & (ids[None, :] < ids[:, None])
    )
    rank = jnp.sum(before.astype(jnp.int32), axis=1)
    order = jnp.sum(jnp.where(rank[None, :] == ids[:, None], ids[None, :], 0), axis=1)
    local_heads = columns // HEAD_DIM
    head_ids = plane * local_heads + jnp.arange(local_heads, dtype=jnp.int32)
    own_ids = core * (half // HEAD_DIM) + head_ids
    other_ids = (1 - core) * (half // HEAD_DIM) + head_ids
    slopes = jnp.exp2(-8.0 * (jnp.concatenate([own_ids, other_ids]) + 1).astype(F32) / HEADS)

    mine_out = lax.dynamic_slice_in_dim(w_out, zero_from(mine_cot), half, 0)
    out_first = gather_first(mine_out)
    tree_unit, _ = normalise(tree.astype(F32))
    normed = (tree_unit * gain_one + shift_one).astype(BF16)
    qkv = (dot_nn(normed, w_heads) + head_shift).astype(BF16)
    qkv, *out_first = gate([qkv, *out_first])
    out_second = gather_second(out_first)
    mixed = attend(order, slopes, qkv)
    mixed, mine_cot, *rest = gate(
        [mixed, mine_cot, *down_pieces, *out_first, *out_second, *up_blocks]
    )
    down_pieces, rest = rest[:groups], rest[groups:]
    out_first, rest = rest[: len(out_first)], rest[len(out_first) :]
    out_second, up_blocks = rest[: len(out_second)], rest[len(out_second) :]
    out_own = place(gather_blocks(mine_out, out_first, out_second), 1)
    up_own = place(up_blocks, 0)
    up_other, out_other = swap_cores(up_own), swap_cores(out_own)

    arrived = [rows_of(mixed, 0)]
    for k in range(1, planes):
        arrived.append(ring_send(rows_of(mixed, k), k))
    cot_first = gather_first(mine_cot)
    down_pieces = list(gate(down_pieces, arrived[1]))
    early = range(1, 3) if groups == 4 else range(1, groups)
    down_blocks = down_pieces[:1] + [xor_send(down_pieces[k], k) for k in early]
    out_other, *rest = gate([out_other, *arrived, *cot_first])
    arrived, cot_first = rest[:planes], rest[planes:]
    cot_second = gather_second(cot_first)
    attended = jnp.stack(arrived[::-1], axis=0)
    attended = jnp.roll(attended, plane + 1, axis=0)
    attended = attended.reshape(planes, rows, 2, columns).transpose(2, 1, 0, 3)
    attended = attended.reshape(2, rows, half)
    middle = mine.astype(F32) + (
        dot_nn(attended[0], out_own) + dot_nn(attended[1], out_other) + out_shift
    )
    unit_two, scale_two = normalise(middle)
    normed_two = (unit_two * gain_two + shift_two).astype(BF16)
    (normed_two,) = gate([normed_two], *cot_second, *down_blocks[1:])
    two_first = gather_first(normed_two)
    rest = gate([*two_first, *down_pieces])
    two_first, down_pieces = rest[: len(two_first)], rest[len(two_first) :]
    two_second = gather_second(two_first)
    down_blocks += [xor_send(down_pieces[k], k) for k in range(len(down_blocks), groups)]
    all_two = jnp.concatenate(gather_blocks(normed_two, two_first, two_second), axis=0)
    all_cot = jnp.concatenate(gather_blocks(mine_cot, cot_first, cot_second), axis=0)

    pre_other = dot_nn(all_two, up_other) + up_shift[1:2]
    active_other = (pre_other * normal_cdf(pre_other)).astype(BF16)
    grad_down = swap_cores(dot_tn(active_other, all_cot).astype(BF16))
    pre_own = dot_nn(all_two, up_own) + up_shift[0:1]
    active_own = (pre_own * normal_cdf(pre_own)).astype(BF16)
    grad_down = (dot_tn(active_own, all_cot) + grad_down.astype(F32)).astype(BF16)

    def slope_of(pre):
        return normal_cdf(pre) + pre * normal_pdf(pre)

    (down_blocks[-1],) = gate(down_blocks[-1:], grad_down)
    down_own = place(down_blocks, 1)
    down_other = swap_cores(down_own)
    back_own = (dot_nt(all_cot, down_own) * slope_of(pre_own)).astype(BF16)
    back_other = (dot_nt(all_cot, down_other) * slope_of(pre_other)).astype(BF16)

    grad_two = (dot_nt(back_own, up_own) + dot_nt(back_other, up_other)).astype(BF16)
    back_other_in = back_other
    back_other, own_two, *sent = gate(
        [back_other] + [grad_two[k * rows : (k + 1) * rows] for k in range(groups)]
    )
    grad_down = lax.psum_scatter(grad_down, "context", scatter_dimension=0, tiled=True)
    grad_two = send_blocks(sent)
    grad_up = swap_cores(dot_tn(all_two, back_other).astype(BF16))
    (grad_up,) = gate([grad_up], grad_two[0])
    grad_up = (dot_tn(all_two, back_own) + grad_up.astype(F32)).astype(BF16)
    grad_up = grad_up.reshape(groups, planes, part // planes, hidden).transpose(1, 0, 2, 3)
    grad_up = grad_up.reshape(width, hidden)
    grad_down, *grad_two = gate([grad_down, *grad_two], grad_up)
    grad_up = lax.psum_scatter(grad_up, "context", scatter_dimension=0, tiled=True)

    grad_two = add_up(own_two, grad_two)
    grad_middle = mine_cot.astype(F32) + norm_back(unit_two, scale_two, gain_two, grad_two)
    grad_branch = grad_middle.astype(BF16)
    grad_mixed = jnp.stack(
        [
            dot_nt(grad_branch, out_own).astype(BF16).reshape(rows, planes, columns),
            dot_nt(grad_branch, out_other).astype(BF16).reshape(rows, planes, columns),
        ],
        axis=1,
    )
    grad_mixed = grad_mixed.transpose(2, 0, 1, 3).reshape(planes, rows, 2 * columns)
    grad_mixed = jnp.roll(grad_mixed, -plane, axis=0)
    grad_out = swap_cores(dot_tn(attended[1], grad_branch).astype(BF16))
    grad_out = dot_tn(attended[0], grad_branch) + grad_out.astype(F32)
    out_own_block, *rest = gate(
        [pick(grad_out, 0, 1)]
        + [pick(grad_out, k, 1).astype(BF16) for k in range(1, groups)]
        + [grad_mixed[k] for k in range(planes)]
    )
    out_blocks, grad_mixed = rest[: groups - 1], rest[groups - 1 :]

    back_rows = [grad_mixed[0]]
    for k in range(1, planes):
        back_rows.append(ring_send(grad_mixed[k], k))
    grad_out = add_up(out_own_block, send_blocks(out_blocks)).astype(BF16)
    grad_tree = jnp.roll(jnp.stack(back_rows[:1] + back_rows[:0:-1]), plane, axis=0)
    grad_tree = grad_tree.reshape(planes * rows, 2 * columns)
    grad_tree, grad_up, grad_down, grad_out = gate([grad_tree, grad_up, grad_down, grad_out])
    grad_out = lax.psum_scatter(grad_out, "context", scatter_dimension=0, tiled=True)

    lines = grad_down.shape[0]
    grad_up = grad_up.reshape(groups, lines // (hidden // part), hidden)
    both = []
    for k in range(groups):
        piece = pick(grad_up, k, 0)[0]
        piece = [piece[:, i : i + part] for i in range(0, hidden, part)]
        both.append(jnp.concatenate([pick(grad_down, k, 1), *piece]))
    both = both[:1] + send_blocks(both[1:])
    grad_qkv = attend_back(order, slopes, qkv, grad_tree)
    grad_qkv, grad_out = gate([grad_qkv, grad_out], *both[1:])
    g_out = lax.all_gather(grad_out, "context", axis=0, tiled=True)
    grad_down = place([piece[None, :lines] for piece in both], 0, zero_from(grad_qkv))
    up_blocks = [piece[lines:] for piece in both]
    down_up, down_down = line_step([grad_down], [grad_down])

    grad_normed = dot_nt(grad_qkv, w_heads)
    head_sums = jnp.sum(grad_qkv.astype(F32), axis=0).reshape(2, pairs, 3, PAIR)
    head_sums = jnp.stack([head_sums[:, :, 0], head_sums[:, :, 2]], axis=1)
    head_row = lax.dynamic_update_slice_in_dim(
        jnp.zeros((2, 2, half), F32), head_sums.reshape(2, 2, columns), plane * columns, 2
    )
    up_sums = [jnp.sum(side.astype(F32), axis=0) for side in (back_own, back_other_in)]
    sums = jnp.concatenate(
        [
            jnp.sum(grad_normed * tree_unit, axis=0),
            jnp.sum(grad_two * unit_two, axis=0),
            jnp.sum(grad_normed, axis=0),
            jnp.sum(grad_two, axis=0),
            jnp.sum(grad_branch.astype(F32), axis=0),
            jnp.sum(mine_cot.astype(F32), axis=0),
            head_row.reshape(-1),
            *up_sums,
        ]
    )
    lines = -(-sums.shape[0] // (16 * width)) * 16
    sums = jnp.pad(sums, (0, lines * width - sums.shape[0])).reshape(lines, width)
    blocks = [
        jnp.concatenate([grad_normed[k * rows : (k + 1) * rows], sums]) for k in range(planes)
    ]
    blocks = jnp.concatenate(blocks).astype(BF16)
    blocks, grad_qkv, down_up[-1], down_down[-1] = gate(
        [blocks, grad_qkv, down_up[-1], down_down[-1]], g_out
    )
    later = zero_from(blocks)
    grad_first = lax.psum_scatter(blocks, "context", scatter_dimension=0, tiled=True)
    upper = up_blocks[0].shape[0]
    up_blocks[0] = lax.dynamic_slice_in_dim(both[0], upper + later, upper, 0)
    g_up = lax.all_gather(jnp.concatenate(up_blocks), "context", axis=0, tiled=True)

    down_up, down_down = line_step(down_up, down_down)
    grad_heads = dot_tn(normed, grad_qkv)
    head_other = swap_cores(grad_heads[:, 3 * columns :].astype(BF16))
    grad_heads = grad_heads[:, : 3 * columns] + head_other.astype(F32)
    head_pieces = [pick(grad_heads, k, 0).astype(BF16) for k in range(1, groups)]
    grad_heads = add_up(pick(grad_heads, 0, 0), send_blocks(head_pieces)).astype(BF16)
    grad_heads = grad_heads.reshape(part, pairs, 3, PAIR).transpose(2, 0, 1, 3)
    grad_heads = grad_heads.reshape(3 * part, columns)
    layer_out = dot_nn(
        lax.dynamic_slice_in_dim(active_own, later, groups * rows, 0), down_own
    ) + dot_nn(lax.dynamic_slice_in_dim(active_other, later, groups * rows, 0), down_other)
    layer_out = layer_out.astype(BF16)
    grad_first, grad_heads, down_up[-1], down_down[-1], *layer_blocks = gate(
        [grad_first, grad_heads, down_up[-1], down_down[-1]]
        + [layer_out[k * rows : (k + 1) * rows] for k in range(groups)]
    )
    while len(down_up) < planes:
        down_up, down_down = line_step(down_up, down_down)
    layer_blocks[1:] = send_blocks(layer_blocks[1:])
    grad_heads, g_up, g_out = gate(
        [grad_heads, g_up, g_out],
        down_up[-1],
        down_down[-1],
        *layer_blocks[1:],
    )
    layer_out = middle + (add_up(layer_blocks[0], layer_blocks[1:]) + down_shift)
    layer_out = both_micros(layer_out.astype(BF16))

    g_heads = lax.all_gather(grad_heads, "context", axis=1, tiled=True)
    ordered = jnp.zeros((part, groups * hidden), F32)
    g_up = g_up.reshape(planes, groups, hidden // part, -1, part)
    for k in range(groups):
        for i in range(hidden // part):
            ordered = lax.dynamic_update_slice_in_dim(
                ordered,
                g_up[:, k, i].reshape(part, part).astype(F32),
                (group ^ k) * hidden + i * part,
                1,
            )
    g_up = ordered
    g_down = jnp.zeros((groups, planes, hidden // planes, part), F32)
    for k, piece in enumerate(line_blocks(down_up, down_down)):
        g_down = lax.dynamic_update_slice_in_dim(
            g_down, piece.astype(F32)[:, None], (plane + k) % planes, 1
        )

    sums = grad_first[rows:].astype(F32).reshape(-1)
    grad_first = grad_first[:rows].astype(F32)
    unit_one, scale_one = normalise(mine.astype(F32))
    grad_tokens = grad_middle + norm_back(unit_one, scale_one, gain_one, grad_first)
    grad_tokens = both_micros(grad_tokens.astype(BF16))

    spread = sums[: 6 * width].reshape(6, groups, part)
    spread = spread.transpose(1, 0, 2).reshape(groups, 6 * part)
    head_row = sums[6 * width : 8 * width].reshape(4, groups, part // 2)
    head_row = head_row.transpose(1, 0, 2).reshape(groups, 2 * part)
    up_sums = sums[8 * width : 8 * width + 2 * hidden].reshape(2, hidden)
    sums = jnp.concatenate([spread, head_row], axis=1)
    total = pick(sums, 0, 0)
    for k in range(1, groups):
        total = total + xor_send(pick(sums, k, 0), k)
    total = total[0]
    total_other = swap_cores(jnp.concatenate([total[: 6 * part], total[7 * part :], up_sums[1]]))
    total = jnp.concatenate([total[: 7 * part], up_sums[0]]) + total_other
    wide = total[: 6 * part].reshape(6, part)
    return (
        layer_out,
        grad_tokens,
        wide[0:2],
        wide[2:4],
        g_heads.astype(F32).reshape(3, part, half),
        total[6 * part : 7 * part].reshape(2, part // 2),
        g_out.astype(F32),
        wide[4],
        g_up,
        total[7 * part :],
        g_down.reshape(groups * hidden, part),
        wide[5],
    )


def solution(mesh):
    rows = P(None, ("fsdp", "context"), None)
    params = (
        P(None, "fsdp"),
        P(None, "fsdp"),
        P(None, "fsdp", "tensor"),
        P(None, ("tensor", "fsdp")),
        P("tensor", "fsdp"),
        P("fsdp"),
        P("fsdp", "tensor"),
        P(("tensor", "fsdp")),
        P("tensor", "fsdp"),
        P("fsdp"),
    )
    in_specs = (rows, rows, P(None, "fsdp"), P(None, "fsdp")) + params
    return jax.shard_map(
        per_device, mesh=mesh, in_specs=in_specs, out_specs=(rows, rows) + params, check_vma=False
    )
```

```python
from functools import partial

import jax
import jax.numpy as jnp
from jax import lax
from jax.experimental import pallas as pl
from jax.experimental.pallas import tpu as pltpu
from jax.sharding import PartitionSpec as P

HEADS = 32
HEAD_DIM = 64
SEG = 128
TREE_SEGS = 8
LAST_DEPTH = 6
MICRO = 2
PAIR = 2 * HEAD_DIM
NEG_FILL = -1e30
F32 = jnp.float32
BF16 = jnp.bfloat16


def dot_nn(left, right):
    return lax.dot_general(left, right, (((1,), (0,)), ((), ())), preferred_element_type=F32)


def dot_tn(left, right):
    return lax.dot_general(left, right, (((0,), (0,)), ((), ())), preferred_element_type=F32)


def dot_nt(left, right):
    return lax.dot_general(left, right, (((1,), (1,)), ((), ())), preferred_element_type=F32)


def swap_cores(value):
    return lax.ppermute(value, "tensor", [(0, 1), (1, 0)])


def xor_send(value, step):
    size = lax.axis_size("fsdp")
    return lax.ppermute(value, "fsdp", [(i, i ^ step) for i in range(size)])


def ring_send(value, step):
    size = lax.axis_size("context")
    return lax.ppermute(value, "context", [(i, (i + step) % size) for i in range(size)])


def line_step(upward, downward):
    size, step = lax.axis_size("context"), len(upward)
    above = lax.ppermute(upward[-1], "context", [(i, i + 1) for i in range(step - 1, size - 1)])
    below = lax.ppermute(downward[-1], "context", [(i + 1, i) for i in range(0, size - step)])
    return upward + [above], downward + [below]


def line_blocks(upward, downward):
    size, index = lax.axis_size("context"), lax.axis_index("context")
    blocks = [upward[0]]
    for k in range(1, size):
        blocks.append(jnp.where(index + k < size, downward[k], upward[size - k]))
    return blocks


def pass_on(*refs):
    pass


def corner(value):
    limits = [1] * (value.ndim - 2) + [8, 128]
    return lax.slice(value, [0] * value.ndim, limits).reshape(8, 128).astype(F32)


def gate(values, *earlier):
    if earlier:
        earlier = (sum([corner(value) for value in earlier[1:]], corner(earlier[0])),)
    anywhere = pl.BlockSpec(memory_space=pl.ANY)
    return pl.pallas_call(
        pass_on,
        out_shape=[jax.ShapeDtypeStruct(value.shape, value.dtype) for value in values],
        in_specs=[anywhere] * (len(values) + len(earlier)),
        out_specs=[anywhere] * len(values),
        input_output_aliases={i: i for i in range(len(values))},
        compiler_params=pltpu.CompilerParams(vmem_limit_bytes=1 << 20),
        cost_estimate=pl.CostEstimate(flops=1, transcendentals=0, bytes_accessed=1),
        name="gate",
    )(*values, *earlier)


def zero_from(value):
    first = value[(slice(0, 1),) * value.ndim].reshape(())
    return jnp.minimum(jnp.abs(first.astype(F32)).astype(jnp.int32), 0)


def gather_first(value):
    size = lax.axis_size("fsdp")
    return [xor_send(value, k) for k in ((1, 2) if size == 4 else range(1, size))]


def gather_second(blocks):
    if lax.axis_size("fsdp") != 4:
        return []
    middle = blocks[0].shape[0] // 2
    return [xor_send(blocks[1][:middle], 1), xor_send(blocks[0][middle:], 2)]


def gather_blocks(value, first, second):
    return [value, *first] + ([jnp.concatenate(second, axis=0)] if second else [])


def place(pieces, axis, offset=0):
    index = lax.axis_index("fsdp")
    width = pieces[0].shape[axis]
    shape = list(pieces[0].shape)
    shape[axis] = width * len(pieces)
    whole = jnp.zeros(shape, pieces[0].dtype)
    for k, piece in enumerate(pieces):
        whole = lax.dynamic_update_slice_in_dim(whole, piece, (index ^ k) * width + offset, axis)
    return whole


def pick(whole, k, axis, offset=0):
    width = whole.shape[axis] // lax.axis_size("fsdp")
    start = (lax.axis_index("fsdp") ^ k) * width + offset
    return lax.dynamic_slice_in_dim(whole, start, width, axis)


def exchange(whole, axis, offset=0):
    blocks = [pick(whole, 0, axis, offset)]
    for k in range(1, lax.axis_size("fsdp")):
        blocks.append(xor_send(pick(whole, k, axis, offset), k))
    return blocks


def send_blocks(pieces):
    return [xor_send(piece, k) for k, piece in enumerate(pieces, 1)]


def add_up(own, pieces):
    return sum([piece.astype(F32) for piece in pieces], own.astype(F32))


def head_lanes(rows):
    return lax.broadcasted_iota(jnp.int32, (rows, PAIR), 1) < HEAD_DIM


def split_heads(value):
    first = head_lanes(value.shape[0])
    zero = jnp.zeros_like(value)
    return jnp.concatenate([jnp.where(first, value, zero), jnp.where(first, zero, value)], axis=0)


def join_heads(stacked):
    first = head_lanes(SEG)
    return jnp.where(first, stacked[:SEG], stacked[SEG:])


def probabilities(stacked_queries, keys, block, slope_a, slope_b):
    width = (block + 1) * SEG
    scores = dot_nt(stacked_queries, keys)
    row = lax.broadcasted_iota(jnp.int32, (2 * SEG, 1), 0)
    column = lax.broadcasted_iota(jnp.int32, (1, width), 1)
    local = jnp.where(row < SEG, row, row - SEG)
    slope = jnp.where(row < SEG, slope_a, slope_b)
    place_row = local + min(block, LAST_DEPTH) * SEG
    place_column = jnp.where(column < (LAST_DEPTH + 1) * SEG, column, column - SEG)
    scores = scores + slope * (place_column - place_row).astype(F32)
    allowed = column <= local + block * SEG
    if block == LAST_DEPTH + 1:
        allowed = allowed & ((column < LAST_DEPTH * SEG) | (column >= (LAST_DEPTH + 1) * SEG))
    scores = jnp.where(allowed, scores, NEG_FILL)
    raised = jnp.exp(scores - jnp.max(scores, axis=-1, keepdims=True))
    return raised * (1.0 / jnp.sum(raised, axis=-1, keepdims=True))


def attention_forward(order, slopes, qkv_ref, out_ref, keys, values):
    pair = pl.program_id(0)
    slope_a, slope_b = slopes[2 * pair], slopes[2 * pair + 1]
    for block in range(TREE_SEGS):
        rows = pl.ds(block * SEG, SEG)
        keys[rows, :] = qkv_ref[order[block], :, PAIR : 2 * PAIR]
        values[rows, :] = qkv_ref[order[block], :, 2 * PAIR : 3 * PAIR]
    for block in range(TREE_SEGS):
        seen = pl.ds(0, (block + 1) * SEG)
        queries = split_heads(qkv_ref[order[block], :, :PAIR] * BF16(HEAD_DIM**-0.5))
        probs = probabilities(queries, keys[seen, :], block, slope_a, slope_b)
        mixed = dot_nn(probs.astype(BF16), values[seen, :])
        out_ref[order[block]] = join_heads(mixed).astype(BF16)


def attention_backward(order, slopes, qkv_ref, grad_ref, out_ref, keys, values, grad_keys, grad_values):
    pair = pl.program_id(0)
    slope_a, slope_b = slopes[2 * pair], slopes[2 * pair + 1]
    for block in range(TREE_SEGS):
        rows = pl.ds(block * SEG, SEG)
        keys[rows, :] = qkv_ref[order[block], :, PAIR : 2 * PAIR]
        values[rows, :] = qkv_ref[order[block], :, 2 * PAIR : 3 * PAIR]
    grad_keys[...] = jnp.zeros_like(grad_keys)
    grad_values[...] = jnp.zeros_like(grad_values)
    for block in range(TREE_SEGS):
        seen = pl.ds(0, (block + 1) * SEG)
        queries = split_heads(qkv_ref[order[block], :, :PAIR] * BF16(HEAD_DIM**-0.5))
        grads = split_heads(grad_ref[order[block]])
        probs = probabilities(queries, keys[seen, :], block, slope_a, slope_b)
        grad_probs = dot_nt(grads, values[seen, :])
        centre = jnp.sum(probs * grad_probs, axis=-1, keepdims=True)
        grad_scores = (probs * (grad_probs - centre)).astype(BF16)
        grad_queries = join_heads(dot_nn(grad_scores, keys[seen, :])) * HEAD_DIM**-0.5
        out_ref[order[block], :, :PAIR] = grad_queries.astype(BF16)
        grad_keys[seen, :] += dot_tn(grad_scores, queries)
        grad_values[seen, :] += dot_tn(probs.astype(BF16), grads)
    for block in range(TREE_SEGS):
        rows = pl.ds(block * SEG, SEG)
        out_ref[order[block], :, PAIR : 2 * PAIR] = grad_keys[rows, :].astype(BF16)
        out_ref[order[block], :, 2 * PAIR : 3 * PAIR] = grad_values[rows, :].astype(BF16)


def block_of(width):
    return pl.BlockSpec((TREE_SEGS, SEG, width), lambda pair, *scalars: (0, 0, pair))


def attend(order, slopes, qkv):
    pairs = qkv.shape[1] // (3 * PAIR)
    rows = TREE_SEGS * SEG
    out = pl.pallas_call(
        attention_forward,
        out_shape=jax.ShapeDtypeStruct((TREE_SEGS, SEG, pairs * PAIR), BF16),
        grid_spec=pltpu.PrefetchScalarGridSpec(
            num_scalar_prefetch=2,
            grid=(pairs,),
            in_specs=[block_of(3 * PAIR)],
            out_specs=block_of(PAIR),
            scratch_shapes=[pltpu.VMEM((rows, PAIR), BF16)] * 2,
        ),
        compiler_params=pltpu.CompilerParams(vmem_limit_bytes=48 << 20),
        cost_estimate=pl.CostEstimate(
            flops=pairs * 32 * rows * rows * PAIR, transcendentals=0, bytes_accessed=1
        ),
        name="attend",
    )(order, slopes, qkv.reshape(TREE_SEGS, SEG, -1))
    return out.reshape(rows, pairs * PAIR)


def attend_back(order, slopes, qkv, grad):
    pairs = qkv.shape[1] // (3 * PAIR)
    rows = TREE_SEGS * SEG
    out = pl.pallas_call(
        attention_backward,
        out_shape=jax.ShapeDtypeStruct((TREE_SEGS, SEG, pairs * 3 * PAIR), BF16),
        grid_spec=pltpu.PrefetchScalarGridSpec(
            num_scalar_prefetch=2,
            grid=(pairs,),
            in_specs=[block_of(3 * PAIR), block_of(PAIR)],
            out_specs=block_of(3 * PAIR),
            scratch_shapes=[pltpu.VMEM((rows, PAIR), BF16)] * 2 + [pltpu.VMEM((rows, PAIR), F32)] * 2,
        ),
        compiler_params=pltpu.CompilerParams(vmem_limit_bytes=48 << 20),
        cost_estimate=pl.CostEstimate(
            flops=pairs * 60 * rows * rows * PAIR, transcendentals=0, bytes_accessed=1
        ),
        name="attend_back",
    )(order, slopes, qkv.reshape(TREE_SEGS, SEG, -1), grad.reshape(TREE_SEGS, SEG, -1))
    return out.reshape(rows, pairs * 3 * PAIR)


def normalise(rows):
    centred = rows - jnp.mean(rows, axis=-1, keepdims=True)
    scale = lax.rsqrt(jnp.mean(centred * centred, axis=-1, keepdims=True) + 1e-05)
    return centred * scale, scale


def norm_back(unit, scale, gain, upstream):
    weighted = upstream * gain
    centre = jnp.mean(weighted, axis=-1, keepdims=True)
    along = jnp.mean(weighted * unit, axis=-1, keepdims=True)
    return scale * (weighted - centre - unit * along)


def normal_cdf(value):
    return 0.5 * (1.0 + lax.erf(value * 0.7071067811865476))


def normal_pdf(value):
    return 0.3989422804014327 * jnp.exp(-0.5 * value * value)


def both_micros(mine):
    other = swap_cores(mine)
    first = lax.axis_index("tensor") == 0
    return jnp.stack([jnp.where(first, mine, other), jnp.where(first, other, mine)])


def per_device(
    tokens,
    cotangent,
    seg_parent,
    positions,
    norm_gain,
    norm_bias,
    w_qkv,
    bias_qv,
    w_out,
    bias_out,
    w_up,
    bias_up,
    w_down,
    bias_down,
):
    planes, groups = lax.axis_size("context"), lax.axis_size("fsdp")
    plane, group, core = (lax.axis_index(name) for name in ("context", "fsdp", "tensor"))
    rows, width = tokens.shape[1], tokens.shape[2]
    part = width // groups
    half = w_qkv.shape[2]
    columns = half // planes
    pairs = columns // PAIR
    hidden = w_up.shape[1] // groups

    def rows_of(whole, k):
        return lax.dynamic_slice_in_dim(whole, ((plane + k) % planes) * rows, rows, 0)

    mine = lax.dynamic_index_in_dim(tokens, core, 0, keepdims=False)
    mine_cot = lax.dynamic_index_in_dim(cotangent, core, 0, keepdims=False)
    packed = jnp.concatenate(
        [
            norm_gain,
            norm_bias,
            bias_out[None],
            bias_down[None],
            bias_qv.reshape(1, part),
            bias_up.reshape(-1, part),
        ],
        axis=0,
    )
    lines = packed.size // (3 * columns)
    chosen = lax.dynamic_slice_in_dim(w_qkv, plane * columns, columns, 2)
    chosen = chosen.reshape(3, part, pairs, PAIR).transpose(1, 2, 0, 3).reshape(part, 3 * columns)
    chosen = jnp.concatenate(
        [
            chosen,
            packed.reshape(lines, 3 * columns),
            jnp.zeros((-lines % 32, 3 * columns), BF16),
        ],
        axis=0,
    )
    up_pieces = [pick(w_up, k, 1) for k in range(groups)]
    down_pieces = [pick(w_down, k, 0) for k in range(groups)]

    tree = lax.all_gather(mine, "context", axis=0, tiled=True)
    head_first = gather_first(chosen)
    up_pieces[1:] = gate(up_pieces[1:], *head_first)
    head_second = gather_second(head_first)
    up_blocks = up_pieces[:1] + send_blocks(up_pieces[1:])
    (mine_cot,) = gate([mine_cot], tree, *head_second)
    head_blocks = gather_blocks(chosen, head_first, head_second)
    heads_own = place([block[:part] for block in head_blocks], 0)
    w_heads = jnp.concatenate([heads_own, swap_cores(heads_own)], axis=1)

    small = [block[part : part + lines].reshape(1, -1, part) for block in head_blocks]
    small = place(small, 0)
    small = jnp.stack([small, swap_cores(small)])
    spread = small[0, :, :6].astype(F32).transpose(1, 0, 2).reshape(6, width)
    gain_one, gain_two, shift_one, shift_two, out_shift, down_shift = (
        spread[i : i + 1] for i in range(6)
    )
    head_shift = small[:, :, 6].astype(F32).reshape(2, groups, 2, part // 2).transpose(0, 2, 1, 3)
    head_shift = lax.dynamic_slice_in_dim(
        head_shift.reshape(2, 2, half), plane * columns, columns, 2
    ).reshape(2, 2, pairs, PAIR)
    head_shift = jnp.stack(
        [head_shift[:, 0], jnp.zeros_like(head_shift[:, 0]), head_shift[:, 1]], axis=2
    ).reshape(1, 2 * pairs * 3 * PAIR)
    up_shift = lax.dynamic_index_in_dim(small, group, 1, keepdims=False)[:, 7:]
    up_shift = up_shift.astype(F32).reshape(2, hidden)

    depth = lax.dynamic_index_in_dim(positions, core, 0, keepdims=False)[::SEG] // SEG
    ids = jnp.arange(TREE_SEGS, dtype=jnp.int32)
    before = (depth[None, :] < depth[:, None]) | (
        (depth[None, :] == depth[:, None]) & (ids[None, :] < ids[:, None])
    )
    rank = jnp.sum(before.astype(jnp.int32), axis=1)
    order = jnp.sum(jnp.where(rank[None, :] == ids[:, None], ids[None, :], 0), axis=1)
    local_heads = columns // HEAD_DIM
    head_ids = plane * local_heads + jnp.arange(local_heads, dtype=jnp.int32)
    own_ids = core * (half // HEAD_DIM) + head_ids
    other_ids = (1 - core) * (half // HEAD_DIM) + head_ids
    slopes = jnp.exp2(-8.0 * (jnp.concatenate([own_ids, other_ids]) + 1).astype(F32) / HEADS)

    mine_out = lax.dynamic_slice_in_dim(w_out, zero_from(mine_cot), half, 0)
    out_first = gather_first(mine_out)
    tree_unit, _ = normalise(tree.astype(F32))
    normed = (tree_unit * gain_one + shift_one).astype(BF16)
    qkv = (dot_nn(normed, w_heads) + head_shift).astype(BF16)
    qkv, *out_first = gate([qkv, *out_first])
    out_second = gather_second(out_first)
    mixed = attend(order, slopes, qkv)
    mixed, mine_cot, *rest = gate(
        [mixed, mine_cot, *out_first, *out_second, *up_blocks]
    )
    out_first, rest = rest[: len(out_first)], rest[len(out_first) :]
    out_second, up_blocks = rest[: len(out_second)], rest[len(out_second) :]
    out_own = place(gather_blocks(mine_out, out_first, out_second), 1)
    up_own = place(up_blocks, 0)
    up_other, out_other = swap_cores(up_own), swap_cores(out_own)

    arrived = [rows_of(mixed, 0)]
    for k in range(1, planes):
        arrived.append(ring_send(rows_of(mixed, k), k))
    cot_first = gather_first(mine_cot)
    down_pieces = list(gate(down_pieces, arrived[1]))
    early = range(1, 3) if groups == 4 else range(1, groups)
    down_blocks = down_pieces[:1] + [xor_send(down_pieces[k], k) for k in early]
    out_other, *rest = gate([out_other, *arrived, *cot_first])
    arrived, cot_first = rest[:planes], rest[planes:]
    cot_second = gather_second(cot_first)
    attended = jnp.stack(arrived[::-1], axis=0)
    attended = jnp.roll(attended, plane + 1, axis=0)
    attended = attended.reshape(planes, rows, 2, columns).transpose(2, 1, 0, 3)
    attended = attended.reshape(2, rows, half)
    middle = mine.astype(F32) + (
        dot_nn(attended[0], out_own) + dot_nn(attended[1], out_other) + out_shift
    )
    unit_two, scale_two = normalise(middle)
    normed_two = (unit_two * gain_two + shift_two).astype(BF16)
    (normed_two,) = gate([normed_two], *cot_second, *down_blocks[1:])
    two_first = gather_first(normed_two)
    rest = gate([*two_first, *down_pieces])
    two_first, down_pieces = rest[: len(two_first)], rest[len(two_first) :]
    two_second = gather_second(two_first)
    down_blocks += [xor_send(down_pieces[k], k) for k in range(len(down_blocks), groups)]
    all_two = jnp.concatenate(gather_blocks(normed_two, two_first, two_second), axis=0)
    all_cot = jnp.concatenate(gather_blocks(mine_cot, cot_first, cot_second), axis=0)

    pre_other = dot_nn(all_two, up_other) + up_shift[1:2]
    active_other = (pre_other * normal_cdf(pre_other)).astype(BF16)
    grad_down = swap_cores(dot_tn(active_other, all_cot).astype(BF16))
    pre_own = dot_nn(all_two, up_own) + up_shift[0:1]
    active_own = (pre_own * normal_cdf(pre_own)).astype(BF16)
    grad_down = (dot_tn(active_own, all_cot) + grad_down.astype(F32)).astype(BF16)

    def slope_of(pre):
        return normal_cdf(pre) + pre * normal_pdf(pre)

    (down_blocks[-1],) = gate(down_blocks[-1:], grad_down)
    down_own = place(down_blocks, 1)
    down_other = swap_cores(down_own)
    back_own = (dot_nt(all_cot, down_own) * slope_of(pre_own)).astype(BF16)
    back_other = (dot_nt(all_cot, down_other) * slope_of(pre_other)).astype(BF16)

    grad_two = (dot_nt(back_own, up_own) + dot_nt(back_other, up_other)).astype(BF16)
    back_other_in = back_other
    back_other, own_two, *sent = gate(
        [back_other] + [grad_two[k * rows : (k + 1) * rows] for k in range(groups)]
    )
    grad_down = lax.psum_scatter(grad_down, "context", scatter_dimension=0, tiled=True)
    grad_two = send_blocks(sent)
    grad_up = swap_cores(dot_tn(all_two, back_other).astype(BF16))
    (grad_up,) = gate([grad_up], grad_two[0])
    grad_up = (dot_tn(all_two, back_own) + grad_up.astype(F32)).astype(BF16)
    grad_up = grad_up.reshape(groups, planes, part // planes, hidden).transpose(1, 0, 2, 3)
    grad_up = grad_up.reshape(width, hidden)
    grad_down, own_two = gate([grad_down, own_two], grad_up, *grad_two)
    grad_up = lax.psum_scatter(grad_up, "context", scatter_dimension=0, tiled=True)

    grad_two = add_up(own_two, grad_two)
    grad_middle = mine_cot.astype(F32) + norm_back(unit_two, scale_two, gain_two, grad_two)
    grad_branch = grad_middle.astype(BF16)
    grad_mixed = jnp.stack(
        [
            dot_nt(grad_branch, out_own).astype(BF16).reshape(rows, planes, columns),
            dot_nt(grad_branch, out_other).astype(BF16).reshape(rows, planes, columns),
        ],
        axis=1,
    )
    grad_mixed = grad_mixed.transpose(2, 0, 1, 3).reshape(planes, rows, 2 * columns)
    grad_mixed = jnp.roll(grad_mixed, -plane, axis=0)
    grad_out = swap_cores(dot_tn(attended[1], grad_branch).astype(BF16))
    grad_out = dot_tn(attended[0], grad_branch) + grad_out.astype(F32)
    out_own_block, *rest = gate(
        [pick(grad_out, 0, 1)]
        + [pick(grad_out, k, 1).astype(BF16) for k in range(1, groups)]
        + [grad_mixed[k] for k in range(planes)]
    )
    out_blocks, grad_mixed = rest[: groups - 1], rest[groups - 1 :]

    back_rows = [grad_mixed[0]]
    for k in range(1, planes):
        back_rows.append(ring_send(grad_mixed[k], k))
    grad_out = add_up(out_own_block, send_blocks(out_blocks)).astype(BF16)
    grad_tree = jnp.roll(jnp.stack(back_rows[:1] + back_rows[:0:-1]), plane, axis=0)
    grad_tree = grad_tree.reshape(planes * rows, 2 * columns)
    grad_tree, grad_up, grad_down, grad_out = gate([grad_tree, grad_up, grad_down, grad_out])
    grad_out = lax.psum_scatter(grad_out, "context", scatter_dimension=0, tiled=True)

    lines = grad_down.shape[0]
    grad_up = grad_up.reshape(groups, lines // (hidden // part), hidden)
    both = []
    for k in range(groups):
        piece = pick(grad_up, k, 0)[0]
        piece = [piece[:, i : i + part] for i in range(0, hidden, part)]
        both.append(jnp.concatenate([pick(grad_down, k, 1), *piece]))
    both = both[:1] + send_blocks(both[1:])
    grad_qkv = attend_back(order, slopes, qkv, grad_tree)
    grad_qkv, grad_out = gate([grad_qkv, grad_out], *both[1:])
    g_out = lax.all_gather(grad_out, "context", axis=0, tiled=True)
    g_up = jnp.concatenate([piece[lines:] for piece in both])
    grad_down = place([piece[None, :lines] for piece in both], 0, zero_from(g_up))
    g_up = lax.all_gather(g_up, "context", axis=0, tiled=True)
    down_up, down_down = line_step([grad_down], [grad_down])

    grad_normed = dot_nt(grad_qkv, w_heads)
    head_sums = jnp.sum(grad_qkv.astype(F32), axis=0).reshape(2, pairs, 3, PAIR)
    head_sums = jnp.stack([head_sums[:, :, 0], head_sums[:, :, 2]], axis=1)
    head_row = lax.dynamic_update_slice_in_dim(
        jnp.zeros((2, 2, half), F32), head_sums.reshape(2, 2, columns), plane * columns, 2
    )
    up_sums = [jnp.sum(side.astype(F32), axis=0) for side in (back_own, back_other_in)]
    sums = jnp.concatenate(
        [
            jnp.sum(grad_normed * tree_unit, axis=0),
            jnp.sum(grad_two * unit_two, axis=0),
            jnp.sum(grad_normed, axis=0),
            jnp.sum(grad_two, axis=0),
            jnp.sum(grad_branch.astype(F32), axis=0),
            jnp.sum(mine_cot.astype(F32), axis=0),
            head_row.reshape(-1),
            *up_sums,
        ]
    )
    lines = -(-sums.shape[0] // (16 * width)) * 16
    sums = jnp.pad(sums, (0, lines * width - sums.shape[0])).reshape(lines, width)
    blocks = [
        jnp.concatenate([grad_normed[k * rows : (k + 1) * rows], sums]) for k in range(planes)
    ]
    blocks = jnp.concatenate(blocks).astype(BF16)
    blocks, grad_qkv, down_up[-1], down_down[-1] = gate(
        [blocks, grad_qkv, down_up[-1], down_down[-1]], g_out
    )
    later = zero_from(blocks)
    grad_first = lax.psum_scatter(blocks, "context", scatter_dimension=0, tiled=True)

    down_up, down_down = line_step(down_up, down_down)
    grad_heads = dot_tn(normed, grad_qkv)
    head_other = swap_cores(grad_heads[:, 3 * columns :].astype(BF16))
    grad_heads = grad_heads[:, : 3 * columns] + head_other.astype(F32)
    head_pieces = [pick(grad_heads, k, 0).astype(BF16) for k in range(1, groups)]
    grad_heads = add_up(pick(grad_heads, 0, 0), send_blocks(head_pieces)).astype(BF16)
    grad_heads = grad_heads.reshape(part, pairs, 3, PAIR).transpose(2, 0, 1, 3)
    grad_heads = grad_heads.reshape(3 * part, columns)
    layer_out = dot_nn(
        lax.dynamic_slice_in_dim(active_own, later, groups * rows, 0), down_own
    ) + dot_nn(lax.dynamic_slice_in_dim(active_other, later, groups * rows, 0), down_other)
    layer_out = layer_out.astype(BF16)
    grad_heads, down_up[-1], down_down[-1], *layer_blocks = gate(
        [grad_heads, down_up[-1], down_down[-1]]
        + [layer_out[k * rows : (k + 1) * rows] for k in range(groups)]
    )
    while len(down_up) < planes:
        down_up, down_down = line_step(down_up, down_down)
    layer_blocks[1:] = send_blocks(layer_blocks[1:])
    grad_first, grad_heads, g_up, g_out = gate(
        [grad_first, grad_heads, g_up, g_out],
        down_up[-1],
        down_down[-1],
        *layer_blocks[1:],
    )
    layer_out = middle + (add_up(layer_blocks[0], layer_blocks[1:]) + down_shift)
    layer_out = both_micros(layer_out.astype(BF16))

    g_heads = lax.all_gather(grad_heads, "context", axis=1, tiled=True)
    ordered = jnp.zeros((part, groups * hidden), F32)
    g_up = g_up.reshape(planes, groups, hidden // part, -1, part)
    for k in range(groups):
        for i in range(hidden // part):
            ordered = lax.dynamic_update_slice_in_dim(
                ordered,
                g_up[:, k, i].reshape(part, part).astype(F32),
                (group ^ k) * hidden + i * part,
                1,
            )
    g_up = ordered
    g_down = jnp.zeros((groups, planes, hidden // planes, part), F32)
    for k, piece in enumerate(line_blocks(down_up, down_down)):
        g_down = lax.dynamic_update_slice_in_dim(
            g_down, piece.astype(F32)[:, None], (plane + k) % planes, 1
        )

    sums = grad_first[rows:].astype(F32).reshape(-1)
    grad_first = grad_first[:rows].astype(F32)
    unit_one, scale_one = normalise(mine.astype(F32))
    grad_tokens = grad_middle + norm_back(unit_one, scale_one, gain_one, grad_first)
    grad_tokens = both_micros(grad_tokens.astype(BF16))

    spread = sums[: 6 * width].reshape(6, groups, part)
    spread = spread.transpose(1, 0, 2).reshape(groups, 6 * part)
    head_row = sums[6 * width : 8 * width].reshape(4, groups, part // 2)
    head_row = head_row.transpose(1, 0, 2).reshape(groups, 2 * part)
    up_sums = sums[8 * width : 8 * width + 2 * hidden].reshape(2, hidden)
    sums = jnp.concatenate([spread, head_row], axis=1)
    total = pick(sums, 0, 0)
    for k in range(1, groups):
        total = total + xor_send(pick(sums, k, 0), k)
    total = total[0]
    total_other = swap_cores(jnp.concatenate([total[: 6 * part], total[7 * part :], up_sums[1]]))
    total = jnp.concatenate([total[: 7 * part], up_sums[0]]) + total_other
    wide = total[: 6 * part].reshape(6, part)
    return (
        layer_out,
        grad_tokens,
        wide[0:2],
        wide[2:4],
        g_heads.astype(F32).reshape(3, part, half),
        total[6 * part : 7 * part].reshape(2, part // 2),
        g_out.astype(F32),
        wide[4],
        g_up,
        total[7 * part :],
        g_down.reshape(groups * hidden, part),
        wide[5],
    )


def solution(mesh):
    rows = P(None, ("fsdp", "context"), None)
    params = (
        P(None, "fsdp"),
        P(None, "fsdp"),
        P(None, "fsdp", "tensor"),
        P(None, ("tensor", "fsdp")),
        P("tensor", "fsdp"),
        P("fsdp"),
        P("fsdp", "tensor"),
        P(("tensor", "fsdp")),
        P("tensor", "fsdp"),
        P("fsdp"),
    )
    in_specs = (rows, rows, P(None, "fsdp"), P(None, "fsdp")) + params
    return jax.shard_map(
        per_device, mesh=mesh, in_specs=in_specs, out_specs=(rows, rows) + params, check_vma=False
    )
```
